256 devices in a mesh: dp: 16 (over z_hi, x, core), space: 16 (over z_lo, y).
Axes of the slice: x: 4, y: 4, z: 8 (z_hi: 2, z_lo: 4; z = z_hi * 4 + z_lo), core: 2. Of those that a mesh axis runs over, the one named last changes fastest.
Arguments:
- volume: bfloat16 [16, 4, 128, 8, 256], P('dp', None, 'space'), may hold values from -6 to 6
- first_filters: bfloat16 [16, 4, 3, 3, 3], replicated, may hold values from -0.625 to 0.625
- first_biases: float32 [16], replicated, may hold values from -0.5 to 0.5
- second_filters: bfloat16 [32, 16, 3, 3, 3], replicated, may hold values from -0.3125 to 0.3125
- second_biases: float32 [32], replicated, may hold values from -0.5 to 0.5
- cotangent: bfloat16 [16, 32, 64, 4, 128], P('dp', None, 'space'), may hold values from -12 to 12
Outputs:
- activations: bfloat16 [16, 32, 64, 4, 128], P('dp', None, 'space')
- pooled_grad: bfloat16 [16, 16, 64, 4, 128], P('dp', None, 'space')
- gradient_one: float32 [16, 4, 3, 3, 3], replicated
- shift_one: float32 [16], replicated
- gradient_two: float32 [32, 16, 3, 3, 3], replicated
- shift_two: float32 [32], replicated
The draws below stay inside these ranges and needn't reach their ends.
All inputs are finite; a program needn't handle non-finite values.
Results may differ from the reference program's by a relative error of at most 0.015.
The reference program's roundings to bfloat16 on the way (of `pooled_one`, `delta_two` and `delta_one`) count: a program that leaves them out, or rounds other values in their place, can miss the bound.
Values may be sent and summed in bfloat16 or wider, within the bound.
No kernel may reach another device: no remote copies, remote signals or barrier semaphores. Data moves between devices by JAX's collectives and lax.ppermute only.
A program may use at most 128 MiB of HBM per device.

```python
import math
import jax
import jax.numpy as jnp
from jax import lax

C_IN = 4
C1 = 16
C2 = 32
HEIGHT = 8
WIDTH = 256
SAMPLES = 16
DEPTH = 128


def draw_cotangent(key, part):
    extent = (SAMPLES, C2, DEPTH // 2, HEIGHT // 2, WIDTH // 2)
    first_key = jax.random.fold_in(key, 0)
    sample_rise = jnp.arange(SAMPLES, dtype=jnp.float32) / max(SAMPLES - 1, 1)
    depth_rise = jnp.arange(DEPTH // 2, dtype=jnp.float32) / max(DEPTH // 2 - 1, 1)
    factor = jnp.exp(math.log(3.0) * (sample_rise[:, None, None, None, None] + depth_rise[None, None, :, None, None] - 1.0))
    values = jax.random.truncated_normal(first_key, -4.0, 4.0, extent, jnp.float32)
    return (values * factor).astype(jnp.bfloat16)


def level_of(rng, dims, cuts, smallest, largest):
    loudness = 1.0
    for dim, parts in cuts:
        heights = jax.random.uniform(jax.random.fold_in(jax.random.fold_in(rng, 6), dim), (parts,), jnp.float32, smallest / len(cuts), largest / len(cuts))
        loudness = loudness * jnp.repeat(jnp.exp(heights), dims[dim] // parts).reshape((-1,) + (1,) * (len(dims) - 1 - dim))
    return loudness


def centred(stream_key, shape, width, limit, cuts=(), kind=jnp.bfloat16):
    entries = width * jax.random.normal(stream_key, shape, jnp.float32)
    if cuts:
        entries = entries * level_of(stream_key, shape, cuts, -0.22, 0.18)
    return jnp.clip(entries, -limit, limit).astype(kind)


def setup_inputs(seed: int = 0) -> dict:
    seeds = jax.random.split(jax.random.key(seed), 7)
    return {
        "volume": centred(seeds[0], (SAMPLES, C_IN, DEPTH, HEIGHT, WIDTH), 1.0, 6.0, ((0, 16), (2, 16))),
        "first_filters": centred(seeds[1], (C1, C_IN, 3, 3, 3), (C_IN * 27) ** -0.5, 0.625),
        "first_biases": jnp.clip(jax.random.uniform(seeds[2], (C1,), jnp.float32, -0.5, 0.5), -0.5, 0.5),
        "second_filters": centred(seeds[3], (C2, C1, 3, 3, 3), (C1 * 27) ** -0.5, 0.3125),
        "second_biases": jnp.clip(jax.random.uniform(seeds[4], (C2,), jnp.float32, -0.5, 0.5), -0.5, 0.5),
        "cotangent": draw_cotangent(jax.random.fold_in(seeds[6], 71), 0),
    }


def convolve(padded, kernel):
    return lax.conv_general_dilated(padded[None].astype(jnp.float32), kernel.astype(jnp.float32), (1, 1, 1), 'VALID', dimension_numbers=('NCDHW', 'OIDHW', 'NCDHW'), precision=lax.Precision.HIGHEST)[0]

def pad_all(values):
    return jnp.pad(values, ((0, 0), (1, 1), (1, 1), (1, 1)))

def leaky_rectify(values):
    return jnp.where(values > 0, values, 0.3 * values)

def rectify_slope(values):
    return jnp.where(values > 0, 1.0, 0.3)

def mean_pool(values):
    extent = values.shape
    blocks = values.reshape(extent[0], extent[1] // 2, 2, extent[2] // 2, 2, extent[3] // 2, 2)
    return lax.optimization_barrier(jnp.sum(blocks, axis=(2, 4, 6))) * 0.125

def spread_up(values):
    extent = values.shape
    grown = jnp.broadcast_to(values[:, :, None, :, None, :, None], (extent[0], extent[1], 2, extent[2], 2, extent[3], 2))
    return grown.reshape(extent[0], 2 * extent[1], 2 * extent[2], 2 * extent[3])

def kernel_grad(padded, errors):
    outs_n = errors.shape[0]
    ins_n = padded.shape[0]
    depth_n, high_n, wide_n = (errors.shape[1], errors.shape[2], errors.shape[3])
    flat_errors = errors.reshape(outs_n, -1).astype(jnp.float32)
    tap_terms = []
    for depth_tap in range(3):
        for height_tap in range(3):
            for width_tap in range(3):
                window = padded[:, depth_tap:depth_tap + depth_n, height_tap:height_tap + high_n, width_tap:width_tap + wide_n]
                window = window.reshape(ins_n, -1).astype(jnp.float32)
                tap_terms.append(jnp.dot(flat_errors, window.T, precision=lax.Precision.HIGHEST))
    stacked = jnp.stack(tap_terms, 0).reshape(3, 3, 3, outs_n, ins_n)
    return stacked.transpose(3, 4, 0, 1, 2)

def reference(volume, first_filters, first_biases, second_filters, second_biases, cotangent):
    flipped = jnp.flip(second_filters, (2, 3, 4)).transpose(1, 0, 2, 3, 4)

    def one_sample(paired):
        sample, target = paired
        first_in = pad_all(sample)
        linear_one = convolve(first_in, first_filters) + first_biases[:, None, None, None]
        pooled_one = mean_pool(leaky_rectify(linear_one)).astype(jnp.bfloat16)
        second_in = pad_all(pooled_one)
        linear_two = convolve(second_in, second_filters) + second_biases[:, None, None, None]
        activations = leaky_rectify(linear_two).astype(jnp.bfloat16)
        delta_two = (target.astype(jnp.float32) * rectify_slope(linear_two)).astype(jnp.bfloat16)
        grad_two = kernel_grad(second_in, delta_two)
        bias_two = lax.optimization_barrier(jnp.sum(delta_two.astype(jnp.float32), axis=(1, 2, 3)))
        pooled_grad = convolve(pad_all(delta_two), flipped).astype(jnp.bfloat16)
        stored_grad = lax.optimization_barrier(pooled_grad)
        delta_one = (spread_up(stored_grad.astype(jnp.float32)) * 0.125 * rectify_slope(linear_one)).astype(jnp.bfloat16)
        grad_one = kernel_grad(first_in, delta_one)
        bias_one = lax.optimization_barrier(jnp.sum(delta_one.astype(jnp.float32), axis=(1, 2, 3)))
        return (activations, pooled_grad, grad_one, bias_one, grad_two, bias_two)
    results = lax.map(one_sample, (volume, cotangent))
    count_one = SAMPLES * DEPTH * HEIGHT * WIDTH
    scale_one = 1.0 / math.sqrt(count_one)
    scale_two = 1.0 / math.sqrt(count_one / 8)
    return (results[0], results[1], lax.optimization_barrier(jnp.sum(results[2], 0)) * scale_one, lax.optimization_barrier(jnp.sum(results[3], 0)) * scale_one, lax.optimization_barrier(jnp.sum(results[4], 0)) * scale_two, lax.optimization_barrier(jnp.sum(results[5], 0)) * scale_two)
```

```python
import math

import jax
import jax.numpy as jnp
from jax import lax
from jax.experimental import pallas as pl
from jax.experimental.pallas import tpu as pltpu
from jax.sharding import PartitionSpec as P

F32 = jnp.float32
BF16 = jnp.bfloat16
HALO = 5
PLANES = 8
LEAK = 0.3


def lanes_dot(left, right):
    return lax.dot_general(left, right, (((1,), (1,)), ((), ())), preferred_element_type=F32)


def plain_dot(left, right):
    return jnp.dot(left, right, preferred_element_type=F32)


def both_shifts(values):
    lane = lax.broadcasted_iota(jnp.int32, values.shape, 1)
    before = jnp.where(lane == 0, 0.0, pltpu.roll(values, 1, 1))
    after = jnp.where(lane == 127, 0.0, pltpu.roll(values, 127, 1))
    return before.astype(BF16), values.astype(BF16), after.astype(BF16)


def layers(
    flags, vol, vol_lo, vol_hi, cot, cot_lo, cot_hi, w1, b1, w2, b2, w3,
    act, pooled_grad, grads,
    split, x1, x2, x3, slope, delta_one, cot_all, cot_below, cot_above, act_all, grad_all, band, thin,
):
    row = lax.broadcasted_iota(jnp.int32, (256, 512), 0)
    col = lax.broadcasted_iota(jnp.int32, (256, 512), 1)
    kind = col // 128
    offset = jnp.where(kind == 0, 0, jnp.where(kind == 1, 1, jnp.where(kind == 2, -1, 2)))
    pick = (row == 2 * (col % 128) + offset).astype(F32).astype(BF16)
    for ci in range(4):
        planes = jnp.concatenate(
            [
                vol_lo[ci].astype(F32),
                vol[ci].astype(F32),
                vol_hi[ci].astype(F32),
                jnp.zeros((2, 8, 256), F32),
            ],
            axis=0,
        )
        parts = plain_dot(planes.reshape(160, 256).astype(BF16), pick)
        for group in range(5):
            for kind_n in range(4):
                split[kind_n, (group * 4 + ci) * 32 : (group * 4 + ci + 1) * 32, :] = parts[
                    group * 32 : group * 32 + 32, kind_n * 128 : kind_n * 128 + 128
                ]
    homes = {0: ((0, 1), (1, 0)), 1: ((0, 2), (1, 1)), 2: ((0, 0),), 3: ((1, 2),)}
    for group in range(5):
        base = group * 144
        x1[base : base + 48, 0:256] = jnp.zeros((48, 256), BF16)
        x1[base + 96 : base + 144, 1792:2048] = jnp.zeros((48, 256), BF16)
    for height in range(8):
        for kind_n in range(4):
            tile = split[kind_n, pl.ds(height, 80, stride=8), :].astype(BF16)
            for kh in range(3):
                out_h = height - kh + 1
                if not 0 <= out_h < 8:
                    continue
                for parity, kw in homes[kind_n]:
                    lane0 = out_h * 256 + parity * 128
                    for group in range(5):
                        row0 = group * 144 + (kh * 3 + kw) * 16
                        x1[row0 : row0 + 16, lane0 : lane0 + 128] = tile[
                            group * 16 : group * 16 + 16
                        ]
    for plane in range(8):
        base = plane * 144
        x2[base : base + 48, 0:128] = jnp.zeros((48, 128), BF16)
        x2[base + 96 : base + 144, 384:512] = jnp.zeros((48, 128), BF16)
    weights_one = w1[...]
    bias_one = b1[...]
    for group in range(4):
        for high in range(4):
            linear = plain_dot(
                weights_one, x1[group * 144 : group * 144 + 288, high * 512 : high * 512 + 512]
            )
            linear = linear + bias_one
            positive = linear > 0
            if group in (1, 2):
                slope[(group - 1) * 64 : group * 64, high * 512 : high * 512 + 512] = jnp.where(
                    positive, 0.125, 0.125 * LEAK
                )
            leaky = jnp.where(positive, linear, LEAK * linear)
            for pair in range(2):
                both = leaky[pair * 32 : pair * 32 + 16] + leaky[pair * 32 + 16 : pair * 32 + 32]
                mean = (
                    (both[:, 0:128] + both[:, 128:256]) + (both[:, 256:384] + both[:, 384:512])
                ) * 0.125
                plane = group * 2 + pair
                if plane < 2:
                    mean = mean * flags[0]
                if plane >= 6:
                    mean = mean * flags[1]
                for kw, moved in enumerate(both_shifts(mean)):
                    for kh in range(3):
                        out_h = high - kh + 1
                        if 0 <= out_h < 4:
                            row0 = plane * 144 + (kh * 3 + kw) * 16
                            x2[row0 : row0 + 16, out_h * 128 : out_h * 128 + 128] = moved
    cot_all[0:512, :] = cot[...].astype(F32)
    cot_below[0:128, :] = cot_lo[...].astype(F32)
    cot_above[0:128, :] = cot_hi[...].astype(F32)
    for plane in range(6):
        base = plane * 288
        x3[base : base + 96, 0:128] = jnp.zeros((96, 128), BF16)
        x3[base + 192 : base + 288, 384:512] = jnp.zeros((96, 128), BF16)
    weights_two = w2[...]
    bias_two = b2[...]
    for plane in range(6):
        linear = plain_dot(weights_two, x2[plane * 144 : plane * 144 + 432, :]) + bias_two
        positive = linear > 0
        factor = jnp.where(positive, 1.0, LEAK)
        leaky = jnp.where(positive, linear, LEAK * linear)
        for high in range(4):
            lanes = slice(high * 128, high * 128 + 128)
            if plane == 0:
                target = cot_below[pl.ds(high, 32, stride=4), :]
            elif plane == 5:
                target = cot_above[pl.ds(high, 32, stride=4), :]
            else:
                at = (plane - 1) * 4 + high
                target = cot_all[pl.ds(at, 32, stride=16), :]
                act_all[pl.ds(at, 32, stride=16), :] = leaky[:, lanes]
            delta = target * factor[:, lanes]
            for kw, moved in enumerate(both_shifts(delta)):
                for kh in range(3):
                    out_h = high - kh + 1
                    if 0 <= out_h < 4:
                        row0 = plane * 288 + (kh * 3 + kw) * 32
                        x3[row0 : row0 + 32, out_h * 128 : out_h * 128 + 128] = moved
    act[...] = act_all[0:512, :].astype(BF16)
    weights_three = w3[...]
    for plane in range(4):
        total = plain_dot(weights_three, x3[plane * 288 : plane * 288 + 864, :])
        for high in range(4):
            tile = total[:, high * 128 : high * 128 + 128].astype(BF16).astype(F32)
            grad_all[pl.ds(plane * 4 + high, 16, stride=16), :] = tile
            for row0 in (plane * 32, plane * 32 + 16):
                for part in range(4):
                    lane0 = high * 512 + part * 128
                    delta_one[row0 : row0 + 16, lane0 : lane0 + 128] = (
                        tile * slope[row0 : row0 + 16, lane0 : lane0 + 128]
                    ).astype(BF16)
    pooled_grad[...] = grad_all[0:256, :].astype(BF16)
    second = jnp.zeros((432, 128), F32)
    shift_two = jnp.zeros((16, 128), F32)
    for plane in range(4):
        delta = jnp.concatenate(
            [x3[(plane + 1) * 288 + 128 : (plane + 1) * 288 + 160, :], jnp.zeros((96, 512), BF16)],
            axis=0,
        )
        second = second + lanes_dot(x2[(plane + 1) * 144 : (plane + 1) * 144 + 432, :], delta)
        shift_two = shift_two + lanes_dot(jnp.ones((16, 512), BF16), delta)
    three = (
        second[0:112] + pltpu.roll(second[112:224], 32, 1) + pltpu.roll(second[224:336], 64, 1)
    )
    grads[0:96, :] = three[0:96] + pltpu.roll(second[336:432], 96, 1)
    grads[96:112, :] = three[96:112]
    first = jnp.zeros((288, 128), F32)
    shift_one = jnp.zeros((16, 128), F32)
    for group in (1, 2):
        delta = jnp.concatenate(
            [delta_one[(group - 1) * 64 : group * 64, :], jnp.zeros((64, 2048), BF16)], axis=0
        )
        first = first + lanes_dot(x1[group * 144 : group * 144 + 288, :], delta)
        shift_one = shift_one + lanes_dot(jnp.ones((16, 2048), BF16), delta)
    band[0:288, :] = first
    lane36 = lax.broadcasted_iota(jnp.int32, (36, 128), 1)
    packed = jnp.zeros((36, 128), F32)
    for kd in range(3):
        total = jnp.zeros((36, 128), F32)
        for plane in range(4):
            at = (plane + kd) // 4 * 144 + (plane + kd) % 4
            piece = band[pl.ds(at, 36, stride=4), :]
            lane0 = (128 + 16 * (kd - plane)) % 128
            total = total + (pltpu.roll(piece, lane0, 1) if lane0 else piece)
        packed = packed + jnp.where((lane36 >= 16 * kd) & (lane36 < 16 * kd + 16), total, 0.0)
    thin[...] = jnp.zeros((48, 128), F32)
    thin[0:36, :] = packed
    grads[112:136, :] = thin[0:24, :] + pltpu.roll(thin[24:48, :], 48, 1)
    lane = lax.broadcasted_iota(jnp.int32, (8, 128), 1)
    ones = shift_one[0:8]
    ones = (
        ones + pltpu.roll(ones, 112, 1) + pltpu.roll(ones, 96, 1) + pltpu.roll(ones, 80, 1)
    )
    ones = jnp.where((lane >= 32) & (lane < 48), pltpu.roll(ones, 32, 1), 0.0)
    grads[136:144, :] = jnp.where(lane < 32, shift_two[0:8], ones)


def unpack(scales, mine, other, grad_one, shift_one, grad_two, shift_two, whole):
    scale_one, scale_two = scales[1], scales[2]
    low = scales[0] > 0
    whole[0:72, :] = jnp.where(low, mine[...], other[...])
    whole[72:144, :] = jnp.where(low, other[...], mine[...])
    for group in range(4):
        rows = whole[0:112, :] * scale_two
        if group:
            rows = pltpu.roll(rows, 128 - 32 * group, 1)
        count = 7 if group < 3 else 6
        for tap in range(count):
            grad_two[group * 7 + tap] = rows[tap * 16 : tap * 16 + 16, 0:32]
    for kd in range(3):
        for tap in range(9):
            at, lane0 = (tap, 0) if tap < 6 else (tap - 6, 48)
            piece = whole[112 + at * 4 : 116 + at * 4, :] * scale_one
            lane0 += 16 * kd
            if lane0:
                piece = pltpu.roll(piece, 128 - lane0, 1)
            grad_one[kd * 9 + tap] = piece[:, 0:16]
    row = whole[136:144, :]
    shift_two[...] = row[0:1, 0:32] * scale_two
    shift_one[...] = pltpu.roll(row, 96, 1)[0:1, 0:16] * scale_one


def in_vmem(count):
    return [pl.BlockSpec(memory_space=pltpu.VMEM)] * count


def run_layers(flags, *arrays):
    return pl.pallas_call(
        layers,
        out_shape=(
            jax.ShapeDtypeStruct((512, 128), BF16),
            jax.ShapeDtypeStruct((256, 128), BF16),
            jax.ShapeDtypeStruct((144, 128), F32),
        ),
        in_specs=[pl.BlockSpec(memory_space=pltpu.SMEM)] + in_vmem(len(arrays)),
        out_specs=tuple(in_vmem(3)),
        scratch_shapes=[
            pltpu.VMEM((4, 648, 128), F32),
            pltpu.VMEM((720, 2048), BF16),
            pltpu.VMEM((1152, 512), BF16),
            pltpu.VMEM((1728, 512), BF16),
            pltpu.VMEM((128, 2048), F32),
            pltpu.VMEM((128, 2048), BF16),
            pltpu.VMEM((528, 128), F32),
            pltpu.VMEM((136, 128), F32),
            pltpu.VMEM((136, 128), F32),
            pltpu.VMEM((528, 128), F32),
            pltpu.VMEM((272, 128), F32),
            pltpu.VMEM((304, 128), F32),
            pltpu.VMEM((48, 128), F32),
        ],
        compiler_params=pltpu.CompilerParams(vmem_limit_bytes=40 << 20),
        name="layers",
    )(flags, *arrays)


def run_unpack(scales, mine, other):
    return pl.pallas_call(
        unpack,
        out_shape=(
            jax.ShapeDtypeStruct((27, 4, 16), F32),
            jax.ShapeDtypeStruct((1, 16), F32),
            jax.ShapeDtypeStruct((27, 16, 32), F32),
            jax.ShapeDtypeStruct((1, 32), F32),
        ),
        in_specs=[pl.BlockSpec(memory_space=pltpu.SMEM)] + in_vmem(2),
        out_specs=tuple(in_vmem(4)),
        scratch_shapes=[pltpu.VMEM((144, 128), F32)],
        name="unpack",
    )(scales, mine, other)


def banded(first_filters):
    taps = first_filters.transpose(2, 3, 4, 1, 0).reshape(3, 9, 4, 16)
    shifted = [jnp.pad(taps, ((j, 5 - j), (0, 0), (0, 0), (0, 0))) for j in range(4)]
    wide = jnp.stack(shifted, 0).reshape(4, 2, 4, 9, 4, 16)
    return wide.transpose(0, 5, 1, 3, 4, 2).reshape(64, 288)


def device_exchanges():
    def place(index):
        dp, space = divmod(index, 16)
        return [dp & 1, (dp >> 1) & 3, space & 3, (dp >> 3) * 4 + (space >> 2)]

    def index_of(core, x, y, z):
        return ((z >> 2) * 8 + x * 2 + core) * 16 + (z & 3) * 4 + y

    def pairing(which, mask):
        pairs = []
        for index in range(256):
            spot = place(index)
            spot[which] ^= mask
            pairs.append((index, index_of(*spot)))
        return pairs

    core = pairing(0, 1)
    others = [pairing(*step) for step in ((2, 1), (2, 3), (1, 1), (1, 3), (3, 1), (3, 2), (3, 7))]
    return core, others


def add_up(grads, core_index):
    axes = ("dp", "space")
    core, others = device_exchanges()
    low = core_index == 0
    top, bottom = grads[:72], grads[72:]
    mine = jnp.where(low, top, bottom) + lax.ppermute(jnp.where(low, bottom, top), axes, core)
    for pairs in others:
        mine = mine + lax.ppermute(mine, axes, pairs)
    return mine, lax.ppermute(mine, axes, core)


def shards(volume, first_filters, first_biases, second_filters, second_biases, cotangent):
    sample, target = volume[0], cotangent[0]
    slabs = lax.axis_size("space")
    here = lax.axis_index("space")
    forward = [(i, i + 1) for i in range(slabs - 1)]
    backward = [(i + 1, i) for i in range(slabs - 1)]
    vol_lo = lax.ppermute(sample[:, PLANES - HALO :], "space", forward)
    vol_hi = lax.ppermute(sample[:, :HALO], "space", backward)
    cot_lo = lax.ppermute(target[:, 3].reshape(128, 128), "space", forward)
    cot_hi = lax.ppermute(target[:, 0].reshape(128, 128), "space", backward)
    w1 = banded(first_filters)
    b1 = jnp.tile(first_biases, 4)[:, None]
    w2 = second_filters.transpose(0, 2, 3, 4, 1).reshape(32, 432)
    w3 = jnp.flip(second_filters, (2, 3, 4)).transpose(1, 2, 3, 4, 0).reshape(16, 864)
    flags = jnp.stack([here > 0, here < slabs - 1]).astype(F32)
    act, pooled_grad, grads = run_layers(
        flags, sample, vol_lo, vol_hi, target.reshape(512, 128), cot_lo, cot_hi,
        w1, b1, w2, second_biases[:, None], w3,
    )
    core_index = lax.axis_index("dp") % 2
    mine, other = add_up(grads, core_index)
    count_one = (
        lax.axis_size("dp") * slabs * PLANES * sample.shape[2] * sample.shape[3]
    )
    scales = jnp.stack(
        [
            (core_index == 0).astype(F32),
            jnp.float32(1.0 / math.sqrt(count_one)),
            jnp.float32(1.0 / math.sqrt(count_one / 8)),
        ]
    )
    grad_one, shift_one, grad_two, shift_two = run_unpack(scales, mine, other)
    return (
        act.reshape(1, 32, 4, 4, 128),
        pooled_grad.reshape(1, 16, 4, 4, 128),
        grad_one.reshape(3, 3, 3, 4, 16).transpose(4, 3, 0, 1, 2),
        shift_one[0],
        grad_two.reshape(3, 3, 3, 16, 32).transpose(4, 3, 0, 1, 2),
        shift_two[0],
    )


def solution(mesh):
    slab = P("dp", None, "space", None, None)
    return jax.shard_map(
        shards,
        mesh=mesh,
        in_specs=(slab, P(), P(), P(), P(), slab),
        out_specs=(slab, slab, P(), P(), P(), P()),
        check_vma=False,
    )
```

```python
import functools
import math

import jax
import jax.numpy as jnp
from jax import lax
from jax.experimental import pallas as pl
from jax.experimental.pallas import tpu as pltpu
from jax.sharding import PartitionSpec as P

F32 = jnp.float32
BF16 = jnp.bfloat16
HALO = 5
PLANES = 8
LEAK = 0.3


def lanes_dot(left, right):
    return lax.dot_general(left, right, (((1,), (1,)), ((), ())), preferred_element_type=F32)


def plain_dot(left, right):
    return jnp.dot(left, right, preferred_element_type=F32)


def both_shifts(values):
    lane = lax.broadcasted_iota(jnp.int32, values.shape, 1)
    before = jnp.where(lane == 0, 0.0, pltpu.roll(values, 1, 1))
    after = jnp.where(lane == 127, 0.0, pltpu.roll(values, 127, 1))
    return before.astype(BF16), values.astype(BF16), after.astype(BF16)


def layers(
    flags, vol, below, above, cot, w1, b1, w2, b2, w3,
    act, pooled_grad, grads,
    split, x1, x2, x3, slope, delta_one, cot_all, act_all, grad_all, band, thin,
):
    row = lax.broadcasted_iota(jnp.int32, (256, 512), 0)
    col = lax.broadcasted_iota(jnp.int32, (256, 512), 1)
    kind = col // 128
    offset = jnp.where(kind == 0, 0, jnp.where(kind == 1, 1, jnp.where(kind == 2, -1, 2)))
    pick = (row == 2 * (col % 128) + offset).astype(F32).astype(BF16)
    for ci in range(4):
        planes = jnp.concatenate(
            [
                below[ci * 40 : ci * 40 + 40, :].astype(F32),
                vol[ci].astype(F32).reshape(64, 256),
                above[ci * 40 : ci * 40 + 40, :].astype(F32),
                jnp.zeros((16, 256), F32),
            ],
            axis=0,
        )
        parts = plain_dot(planes.astype(BF16), pick)
        for group in range(5):
            for kind_n in range(4):
                split[kind_n, (group * 4 + ci) * 32 : (group * 4 + ci + 1) * 32, :] = parts[
                    group * 32 : group * 32 + 32, kind_n * 128 : kind_n * 128 + 128
                ]
    homes = {0: ((0, 1), (1, 0)), 1: ((0, 2), (1, 1)), 2: ((0, 0),), 3: ((1, 2),)}
    for group in range(5):
        base = group * 144
        x1[base : base + 48, 0:256] = jnp.zeros((48, 256), BF16)
        x1[base + 96 : base + 144, 1792:2048] = jnp.zeros((48, 256), BF16)
    for height in range(8):
        for kind_n in range(4):
            tile = split[kind_n, pl.ds(height, 80, stride=8), :].astype(BF16)
            for kh in range(3):
                out_h = height - kh + 1
                if not 0 <= out_h < 8:
                    continue
                for parity, kw in homes[kind_n]:
                    lane0 = out_h * 256 + parity * 128
                    for group in range(5):
                        row0 = group * 144 + (kh * 3 + kw) * 16
                        x1[row0 : row0 + 16, lane0 : lane0 + 128] = tile[
                            group * 16 : group * 16 + 16
                        ]
    for plane in range(8):
        base = plane * 144
        x2[base : base + 48, 0:128] = jnp.zeros((48, 128), BF16)
        x2[base + 96 : base + 144, 384:512] = jnp.zeros((48, 128), BF16)
    weights_one = w1[...]
    bias_one = b1[...]
    for group in range(4):
        for high in range(4):
            linear = plain_dot(
                weights_one, x1[group * 144 : group * 144 + 288, high * 512 : high * 512 + 512]
            )
            linear = linear + bias_one
            positive = linear > 0
            if group in (1, 2):
                slope[(group - 1) * 64 : group * 64, high * 512 : high * 512 + 512] = jnp.where(
                    positive, 0.125, 0.125 * LEAK
                )
            leaky = jnp.where(positive, linear, LEAK * linear)
            for pair in range(2):
                both = leaky[pair * 32 : pair * 32 + 16] + leaky[pair * 32 + 16 : pair * 32 + 32]
                mean = (
                    (both[:, 0:128] + both[:, 128:256]) + (both[:, 256:384] + both[:, 384:512])
                ) * 0.125
                plane = group * 2 + pair
                if plane < 2:
                    mean = mean * flags[0]
                if plane >= 6:
                    mean = mean * flags[1]
                for kw, moved in enumerate(both_shifts(mean)):
                    for kh in range(3):
                        out_h = high - kh + 1
                        if 0 <= out_h < 4:
                            row0 = plane * 144 + (kh * 3 + kw) * 16
                            x2[row0 : row0 + 16, out_h * 128 : out_h * 128 + 128] = moved
    cot_all[0:512, :] = cot[...].astype(F32)
    for plane in range(6):
        base = plane * 288
        x3[base : base + 96, 0:128] = jnp.zeros((96, 128), BF16)
        x3[base + 192 : base + 288, 384:512] = jnp.zeros((96, 128), BF16)
    weights_two = w2[...]
    bias_two = b2[...]
    for plane in range(6):
        linear = plain_dot(weights_two, x2[plane * 144 : plane * 144 + 432, :]) + bias_two
        positive = linear > 0
        factor = jnp.where(positive, 1.0, LEAK)
        leaky = jnp.where(positive, linear, LEAK * linear)
        for high in range(4):
            lanes = slice(high * 128, high * 128 + 128)
            if plane in (0, 5):
                outer = below if plane == 0 else above
                row0, lane0 = 160 + high // 2 * 32, high % 2 * 128
                target = outer[row0 : row0 + 32, lane0 : lane0 + 128].astype(F32)
            else:
                at = (plane - 1) * 4 + high
                target = cot_all[pl.ds(at, 32, stride=16), :]
                act_all[pl.ds(at, 32, stride=16), :] = leaky[:, lanes]
            delta = target * factor[:, lanes]
            for kw, moved in enumerate(both_shifts(delta)):
                for kh in range(3):
                    out_h = high - kh + 1
                    if 0 <= out_h < 4:
                        row0 = plane * 288 + (kh * 3 + kw) * 32
                        x3[row0 : row0 + 32, out_h * 128 : out_h * 128 + 128] = moved
    act[...] = act_all[0:512, :].astype(BF16)
    weights_three = w3[:, 0:864]
    for plane in range(4):
        total = plain_dot(weights_three, x3[plane * 288 : plane * 288 + 864, :])
        for high in range(4):
            tile = total[:, high * 128 : high * 128 + 128].astype(BF16).astype(F32)
            grad_all[pl.ds(plane * 4 + high, 16, stride=16), :] = tile
            for row0 in (plane * 32, plane * 32 + 16):
                for part in range(4):
                    lane0 = high * 512 + part * 128
                    delta_one[row0 : row0 + 16, lane0 : lane0 + 128] = (
                        tile * slope[row0 : row0 + 16, lane0 : lane0 + 128]
                    ).astype(BF16)
    pooled_grad[...] = grad_all[0:256, :].astype(BF16)
    second = jnp.zeros((432, 128), F32)
    shift_two = jnp.zeros((16, 128), F32)
    for plane in range(4):
        delta = jnp.concatenate(
            [x3[(plane + 1) * 288 + 128 : (plane + 1) * 288 + 160, :], jnp.zeros((96, 512), BF16)],
            axis=0,
        )
        second = second + lanes_dot(x2[(plane + 1) * 144 : (plane + 1) * 144 + 432, :], delta)
        shift_two = shift_two + lanes_dot(jnp.ones((16, 512), BF16), delta)
    three = (
        second[0:112] + pltpu.roll(second[112:224], 32, 1) + pltpu.roll(second[224:336], 64, 1)
    )
    grads[0:96, :] = three[0:96] + pltpu.roll(second[336:432], 96, 1)
    grads[96:112, :] = three[96:112]
    first = jnp.zeros((288, 128), F32)
    shift_one = jnp.zeros((16, 128), F32)
    for group in (1, 2):
        delta = jnp.concatenate(
            [delta_one[(group - 1) * 64 : group * 64, :], jnp.zeros((64, 2048), BF16)], axis=0
        )
        first = first + lanes_dot(x1[group * 144 : group * 144 + 288, :], delta)
        shift_one = shift_one + lanes_dot(jnp.ones((16, 2048), BF16), delta)
    band[0:288, :] = first
    lane36 = lax.broadcasted_iota(jnp.int32, (36, 128), 1)
    packed = jnp.zeros((36, 128), F32)
    for kd in range(3):
        total = jnp.zeros((36, 128), F32)
        for plane in range(4):
            at = (plane + kd) // 4 * 144 + (plane + kd) % 4
            piece = band[pl.ds(at, 36, stride=4), :]
            lane0 = (128 + 16 * (kd - plane)) % 128
            total = total + (pltpu.roll(piece, lane0, 1) if lane0 else piece)
        packed = packed + jnp.where((lane36 >= 16 * kd) & (lane36 < 16 * kd + 16), total, 0.0)
    thin[...] = jnp.zeros((48, 128), F32)
    thin[0:36, :] = packed
    grads[112:136, :] = thin[0:24, :] + pltpu.roll(thin[24:48, :], 48, 1)
    lane = lax.broadcasted_iota(jnp.int32, (8, 128), 1)
    ones = shift_one[0:8]
    ones = (
        ones + pltpu.roll(ones, 112, 1) + pltpu.roll(ones, 96, 1) + pltpu.roll(ones, 80, 1)
    )
    ones = jnp.where((lane >= 32) & (lane < 48), pltpu.roll(ones, 32, 1), 0.0)
    grads[136:144, :] = jnp.where(lane < 32, shift_two[0:8], ones)


def edges(vol, cot, upward, downward, cot_all):
    cot_all[0:512, :] = cot[...].astype(F32)
    for out, first, plane in ((upward, PLANES - HALO, 3), (downward, 0, 0)):
        for ci in range(4):
            block = vol[ci, first : first + HALO].astype(F32).reshape(40, 256)
            out[ci * 40 : ci * 40 + 40, :] = block.astype(BF16)
        for high in range(4):
            row0, lane0 = 160 + high // 2 * 32, high % 2 * 128
            tile = cot_all[pl.ds(plane * 4 + high, 32, stride=16), :]
            out[row0 : row0 + 32, lane0 : lane0 + 128] = tile.astype(BF16)


def column(row, height):
    count = row.shape[1]
    at = lax.broadcasted_iota(jnp.int32, (height, count), 0) % count
    lane = lax.broadcasted_iota(jnp.int32, (height, count), 1)
    return jnp.sum(jnp.where(at == lane, row, 0.0), axis=1, keepdims=True)


def prepare(first, bias_one, second, bias_two, w1, b1, w2, b2, w3, wide_one, wide_two, bands):
    b1[...] = column(bias_one[...], 64)
    b2[...] = column(bias_two[...], 32)
    wide_one[...] = jnp.zeros((112, 128), F32)
    wide_one[0:108, 0:16] = first[...].astype(F32)
    bands[...] = jnp.zeros((384, 128), F32)
    for at in range(6):
        total = jnp.zeros((36, 128), F32)
        for kd in range(3):
            j = at - kd
            if 0 <= j < 4:
                piece = wide_one[kd * 36 : kd * 36 + 36, :]
                total = total + (pltpu.roll(piece, 16 * j, 1) if j else piece)
        bands[pl.ds(at // 4 * 144 + at % 4, 36, stride=4), :] = total
    w1[...] = bands[...].T[0:64, 0:288].astype(BF16)
    wide_two[...] = jnp.zeros((512, 128), F32)
    wide_two[0:432, 0:32] = second[...].astype(F32)
    w2[...] = wide_two[...].T[0:32, 0:432].astype(BF16)
    for quad in range(7):
        total = wide_two[(26 - quad * 4) * 16 : (26 - quad * 4) * 16 + 16, :]
        for k in range(1, 4):
            tap = 26 - quad * 4 - k
            if tap >= 0:
                total = total + pltpu.roll(wide_two[tap * 16 : tap * 16 + 16, :], 32 * k, 1)
        w3[:, quad * 128 : quad * 128 + 128] = total.astype(BF16)


def unpack(scale_one, scale_two, core, mine, other, grad_one, shift_one, grad_two, shift_two, whole):
    low = core[0] == 0
    whole[0:72, :] = jnp.where(low, mine[...], other[...])
    whole[72:144, :] = jnp.where(low, other[...], mine[...])
    for group in range(4):
        rows = whole[0:112, :] * scale_two
        if group:
            rows = pltpu.roll(rows, 128 - 32 * group, 1)
        count = 7 if group < 3 else 6
        for tap in range(count):
            grad_two[group * 7 + tap] = rows[tap * 16 : tap * 16 + 16, 0:32]
    for kd in range(3):
        for tap in range(9):
            at, lane0 = (tap, 0) if tap < 6 else (tap - 6, 48)
            piece = whole[112 + at * 4 : 116 + at * 4, :] * scale_one
            lane0 += 16 * kd
            if lane0:
                piece = pltpu.roll(piece, 128 - lane0, 1)
            grad_one[kd * 9 + tap] = piece[:, 0:16]
    row = whole[136:144, :]
    shift_two[...] = row[0:1, 0:32] * scale_two
    shift_one[...] = pltpu.roll(row, 96, 1)[0:1, 0:16] * scale_one


def in_vmem(count):
    return [pl.BlockSpec(memory_space=pltpu.VMEM)] * count


def run_layers(flags, *arrays):
    return pl.pallas_call(
        layers,
        out_shape=(
            jax.ShapeDtypeStruct((512, 128), BF16),
            jax.ShapeDtypeStruct((256, 128), BF16),
            jax.ShapeDtypeStruct((144, 128), F32),
        ),
        in_specs=[pl.BlockSpec(memory_space=pltpu.SMEM)] + in_vmem(len(arrays)),
        out_specs=tuple(in_vmem(3)),
        scratch_shapes=[
            pltpu.VMEM((4, 648, 128), F32),
            pltpu.VMEM((720, 2048), BF16),
            pltpu.VMEM((1152, 512), BF16),
            pltpu.VMEM((1728, 512), BF16),
            pltpu.VMEM((128, 2048), F32),
            pltpu.VMEM((128, 2048), BF16),
            pltpu.VMEM((528, 128), F32),
            pltpu.VMEM((528, 128), F32),
            pltpu.VMEM((272, 128), F32),
            pltpu.VMEM((304, 128), F32),
            pltpu.VMEM((48, 128), F32),
        ],
        compiler_params=pltpu.CompilerParams(vmem_limit_bytes=24 << 20),
        name="layers",
    )(flags, *arrays)


def run_edges(sample, target):
    return pl.pallas_call(
        edges,
        out_shape=(jax.ShapeDtypeStruct((224, 256), BF16),) * 2,
        in_specs=in_vmem(2),
        out_specs=tuple(in_vmem(2)),
        scratch_shapes=[pltpu.VMEM((528, 128), F32)],
        compiler_params=pltpu.CompilerParams(vmem_limit_bytes=4 << 20),
        name="edges",
    )(sample, target)


def run_prepare(*filters):
    return pl.pallas_call(
        prepare,
        out_shape=(
            jax.ShapeDtypeStruct((64, 288), BF16),
            jax.ShapeDtypeStruct((64, 1), F32),
            jax.ShapeDtypeStruct((32, 432), BF16),
            jax.ShapeDtypeStruct((32, 1), F32),
            jax.ShapeDtypeStruct((16, 896), BF16),
        ),
        in_specs=in_vmem(4),
        out_specs=tuple(in_vmem(5)),
        scratch_shapes=[
            pltpu.VMEM((112, 128), F32),
            pltpu.VMEM((512, 128), F32),
            pltpu.VMEM((384, 128), F32),
        ],
        compiler_params=pltpu.CompilerParams(vmem_limit_bytes=4 << 20),
        name="prepare",
    )(*filters)


def run_unpack(scales, core_index, mine, other):
    return pl.pallas_call(
        functools.partial(unpack, *scales),
        out_shape=(
            jax.ShapeDtypeStruct((27, 4, 16), F32),
            jax.ShapeDtypeStruct((1, 16), F32),
            jax.ShapeDtypeStruct((27, 16, 32), F32),
            jax.ShapeDtypeStruct((1, 32), F32),
        ),
        in_specs=[pl.BlockSpec(memory_space=pltpu.SMEM)] + in_vmem(2),
        out_specs=tuple(in_vmem(4)),
        scratch_shapes=[pltpu.VMEM((144, 128), F32)],
        compiler_params=pltpu.CompilerParams(vmem_limit_bytes=4 << 20),
        name="unpack",
    )(core_index, mine, other)


def device_exchanges():
    def place(index):
        dp, space = divmod(index, 16)
        return [dp & 1, (dp >> 1) & 3, space & 3, (dp >> 3) * 4 + (space >> 2)]

    def index_of(core, x, y, z):
        return ((z >> 2) * 8 + x * 2 + core) * 16 + (z & 3) * 4 + y

    def pairing(which, mask):
        pairs = []
        for index in range(256):
            spot = place(index)
            spot[which] ^= mask
            pairs.append((index, index_of(*spot)))
        return pairs

    core = pairing(0, 1)
    others = [pairing(*step) for step in ((2, 1), (2, 2), (1, 1), (1, 2), (3, 1), (3, 2), (3, 7))]
    return core, others


def add_up(grads, core_index):
    axes = ("dp", "space")
    core, others = device_exchanges()
    low = core_index == 0
    top, bottom = grads[:72], grads[72:]
    mine = jnp.where(low, top, bottom) + lax.ppermute(jnp.where(low, bottom, top), axes, core)
    for pairs in others:
        mine = mine + lax.ppermute(mine, axes, pairs)
    return mine, lax.ppermute(mine, axes, core)


def as_rows(first_filters, first_biases, second_filters, second_biases):
    return (
        first_filters.transpose(2, 3, 4, 1, 0).reshape(108, 16),
        first_biases[None],
        second_filters.transpose(2, 3, 4, 1, 0).reshape(432, 32),
        second_biases[None],
    )


def shards(volume, first_filters, first_biases, second_filters, second_biases, cotangent):
    sample, target = volume[0], cotangent[0]
    slabs = lax.axis_size("space")
    here = lax.axis_index("space")
    forward = [(i, i + 1) for i in range(slabs - 1)]
    backward = [(i + 1, i) for i in range(slabs - 1)]
    target = target.reshape(512, 128)
    upward, downward = run_edges(sample, target)
    below = lax.ppermute(upward, "space", forward)
    above = lax.ppermute(downward, "space", backward)
    matrices = run_prepare(*as_rows(first_filters, first_biases, second_filters, second_biases))
    flags = jnp.stack([here > 0, here < slabs - 1]).astype(F32)
    act, pooled_grad, grads = run_layers(flags, sample, below, above, target, *matrices)
    core_index = lax.axis_index("dp") % 2
    mine, other = add_up(grads, core_index)
    count_one = (
        lax.axis_size("dp") * slabs * PLANES * sample.shape[2] * sample.shape[3]
    )
    scales = (1.0 / math.sqrt(count_one), 1.0 / math.sqrt(count_one / 8))
    grad_one, shift_one, grad_two, shift_two = run_unpack(scales, core_index[None], mine, other)
    return (
        act.reshape(1, 32, 4, 4, 128),
        pooled_grad.reshape(1, 16, 4, 4, 128),
        grad_one.reshape(3, 3, 3, 4, 16).transpose(4, 3, 0, 1, 2),
        shift_one[0],
        grad_two.reshape(3, 3, 3, 16, 32).transpose(4, 3, 0, 1, 2),
        shift_two[0],
    )


def solution(mesh):
    slab = P("dp", None, "space", None, None)
    return jax.shard_map(
        shards,
        mesh=mesh,
        in_specs=(slab, P(), P(), P(), P(), slab),
        out_specs=(slab, slab, P(), P(), P(), P()),
        check_vma=False,
    )
```

```python
import functools
import math

import jax
import jax.numpy as jnp
from jax import lax
from jax.experimental import pallas as pl
from jax.experimental.pallas import tpu as pltpu
from jax.sharding import PartitionSpec as P

F32 = jnp.float32
BF16 = jnp.bfloat16
HALO = 5
PLANES = 8
LEAK = 0.3


def lanes_dot(left, right):
    return lax.dot_general(left, right, (((1,), (1,)), ((), ())), preferred_element_type=F32)


def plain_dot(left, right):
    return jnp.dot(left, right, preferred_element_type=F32)


def both_shifts(values):
    lane = lax.broadcasted_iota(jnp.int32, values.shape, 1)
    before = jnp.where(lane == 0, 0.0, pltpu.roll(values, 1, 1))
    after = jnp.where(lane == 127, 0.0, pltpu.roll(values, 127, 1))
    return before.astype(BF16), values.astype(BF16), after.astype(BF16)


def layers(
    flags, vol, below, above, cot, w1, b1, w2, b2, w3,
    act, pooled_grad, grads,
    split, x1, x2, x3, slope, delta_one, cot_all, act_all, grad_all, band, thin,
):
    row = lax.broadcasted_iota(jnp.int32, (256, 512), 0)
    col = lax.broadcasted_iota(jnp.int32, (256, 512), 1)
    kind = col // 128
    offset = jnp.where(kind == 0, 0, jnp.where(kind == 1, 1, jnp.where(kind == 2, -1, 2)))
    pick = (row == 2 * (col % 128) + offset).astype(F32).astype(BF16)
    for ci in range(4):
        planes = jnp.concatenate(
            [
                below[ci * HALO : ci * HALO + HALO].astype(F32).reshape(40, 256),
                vol[ci].astype(F32).reshape(64, 256),
                above[ci * HALO : ci * HALO + HALO].astype(F32).reshape(40, 256),
                jnp.zeros((16, 256), F32),
            ],
            axis=0,
        )
        parts = plain_dot(planes.astype(BF16), pick)
        for group in range(5):
            for kind_n in range(4):
                split[kind_n, (group * 4 + ci) * 32 : (group * 4 + ci + 1) * 32, :] = parts[
                    group * 32 : group * 32 + 32, kind_n * 128 : kind_n * 128 + 128
                ]
    homes = {0: ((0, 1), (1, 0)), 1: ((0, 2), (1, 1)), 2: ((0, 0),), 3: ((1, 2),)}
    for group in range(5):
        base = group * 144
        x1[base : base + 48, 0:256] = jnp.zeros((48, 256), BF16)
        x1[base + 96 : base + 144, 1792:2048] = jnp.zeros((48, 256), BF16)
    for height in range(8):
        for kind_n in range(4):
            tile = split[kind_n, pl.ds(height, 80, stride=8), :].astype(BF16)
            for kh in range(3):
                out_h = height - kh + 1
                if not 0 <= out_h < 8:
                    continue
                for parity, kw in homes[kind_n]:
                    lane0 = out_h * 256 + parity * 128
                    for group in range(5):
                        row0 = group * 144 + (kh * 3 + kw) * 16
                        x1[row0 : row0 + 16, lane0 : lane0 + 128] = tile[
                            group * 16 : group * 16 + 16
                        ]
    for plane in range(8):
        base = plane * 144
        x2[base : base + 48, 0:128] = jnp.zeros((48, 128), BF16)
        x2[base + 96 : base + 144, 384:512] = jnp.zeros((48, 128), BF16)
    weights_one = w1[...]
    bias_one = b1[...]
    for group in range(4):
        for high in range(4):
            linear = plain_dot(
                weights_one, x1[group * 144 : group * 144 + 288, high * 512 : high * 512 + 512]
            )
            linear = linear + bias_one
            positive = linear > 0
            if group in (1, 2):
                slope[(group - 1) * 64 : group * 64, high * 512 : high * 512 + 512] = jnp.where(
                    positive, 0.125, 0.125 * LEAK
                )
            leaky = jnp.where(positive, linear, LEAK * linear)
            for pair in range(2):
                both = leaky[pair * 32 : pair * 32 + 16] + leaky[pair * 32 + 16 : pair * 32 + 32]
                mean = (
                    (both[:, 0:128] + both[:, 128:256]) + (both[:, 256:384] + both[:, 384:512])
                ) * 0.125
                plane = group * 2 + pair
                if plane < 2:
                    mean = mean * flags[0]
                if plane >= 6:
                    mean = mean * flags[1]
                for kw, moved in enumerate(both_shifts(mean)):
                    for kh in range(3):
                        out_h = high - kh + 1
                        if 0 <= out_h < 4:
                            row0 = plane * 144 + (kh * 3 + kw) * 16
                            x2[row0 : row0 + 16, out_h * 128 : out_h * 128 + 128] = moved
    cot_all[0:512, :] = cot[...].astype(F32)
    for plane in range(6):
        base = plane * 288
        x3[base : base + 96, 0:128] = jnp.zeros((96, 128), BF16)
        x3[base + 192 : base + 288, 384:512] = jnp.zeros((96, 128), BF16)
    weights_two = w2[...]
    bias_two = b2[...]
    for plane in range(6):
        linear = plain_dot(weights_two, x2[plane * 144 : plane * 144 + 432, :]) + bias_two
        positive = linear > 0
        factor = jnp.where(positive, 1.0, LEAK)
        leaky = jnp.where(positive, linear, LEAK * linear)
        for high in range(4):
            lanes = slice(high * 128, high * 128 + 128)
            if plane in (0, 5):
                outer = below if plane == 0 else above
                block, lane0 = 20 + high // 2 * 4, high % 2 * 128
                target = outer[block : block + 4, :, lane0 : lane0 + 128].astype(F32)
                target = target.reshape(32, 128)
            else:
                at = (plane - 1) * 4 + high
                target = cot_all[pl.ds(at, 32, stride=16), :]
                act_all[pl.ds(at, 32, stride=16), :] = leaky[:, lanes]
            delta = target * factor[:, lanes]
            for kw, moved in enumerate(both_shifts(delta)):
                for kh in range(3):
                    out_h = high - kh + 1
                    if 0 <= out_h < 4:
                        row0 = plane * 288 + (kh * 3 + kw) * 32
                        x3[row0 : row0 + 32, out_h * 128 : out_h * 128 + 128] = moved
    act[...] = act_all[0:512, :].astype(BF16)
    weights_three = w3[:, 0:864]
    for plane in range(4):
        total = plain_dot(weights_three, x3[plane * 288 : plane * 288 + 864, :])
        for high in range(4):
            tile = total[:, high * 128 : high * 128 + 128].astype(BF16).astype(F32)
            grad_all[pl.ds(plane * 4 + high, 16, stride=16), :] = tile
            for row0 in (plane * 32, plane * 32 + 16):
                for part in range(4):
                    lane0 = high * 512 + part * 128
                    delta_one[row0 : row0 + 16, lane0 : lane0 + 128] = (
                        tile * slope[row0 : row0 + 16, lane0 : lane0 + 128]
                    ).astype(BF16)
    pooled_grad[...] = grad_all[0:256, :].astype(BF16)
    second = jnp.zeros((432, 128), F32)
    shift_two = jnp.zeros((16, 128), F32)
    for plane in range(4):
        delta = jnp.concatenate(
            [x3[(plane + 1) * 288 + 128 : (plane + 1) * 288 + 160, :], jnp.zeros((96, 512), BF16)],
            axis=0,
        )
        second = second + lanes_dot(x2[(plane + 1) * 144 : (plane + 1) * 144 + 432, :], delta)
        shift_two = shift_two + lanes_dot(jnp.ones((16, 512), BF16), delta)
    three = (
        second[0:112] + pltpu.roll(second[112:224], 32, 1) + pltpu.roll(second[224:336], 64, 1)
    )
    grads[0:96, :] = three[0:96] + pltpu.roll(second[336:432], 96, 1)
    grads[96:112, :] = three[96:112]
    first = jnp.zeros((288, 128), F32)
    shift_one = jnp.zeros((16, 128), F32)
    for group in (1, 2):
        delta = jnp.concatenate(
            [delta_one[(group - 1) * 64 : group * 64, :], jnp.zeros((64, 2048), BF16)], axis=0
        )
        first = first + lanes_dot(x1[group * 144 : group * 144 + 288, :], delta)
        shift_one = shift_one + lanes_dot(jnp.ones((16, 2048), BF16), delta)
    band[0:288, :] = first
    lane36 = lax.broadcasted_iota(jnp.int32, (36, 128), 1)
    packed = jnp.zeros((36, 128), F32)
    for kd in range(3):
        total = jnp.zeros((36, 128), F32)
        for plane in range(4):
            at = (plane + kd) // 4 * 144 + (plane + kd) % 4
            piece = band[pl.ds(at, 36, stride=4), :]
            lane0 = (128 + 16 * (kd - plane)) % 128
            total = total + (pltpu.roll(piece, lane0, 1) if lane0 else piece)
        packed = packed + jnp.where((lane36 >= 16 * kd) & (lane36 < 16 * kd + 16), total, 0.0)
    thin[...] = jnp.zeros((48, 128), F32)
    thin[0:36, :] = packed
    grads[112:136, :] = thin[0:24, :] + pltpu.roll(thin[24:48, :], 48, 1)
    lane = lax.broadcasted_iota(jnp.int32, (8, 128), 1)
    ones = shift_one[0:8]
    ones = (
        ones + pltpu.roll(ones, 112, 1) + pltpu.roll(ones, 96, 1) + pltpu.roll(ones, 80, 1)
    )
    ones = jnp.where((lane >= 32) & (lane < 48), pltpu.roll(ones, 32, 1), 0.0)
    grads[136:144, :] = jnp.where(lane < 32, shift_two[0:8], ones)


def edges(vol, cot, upward, downward, cot_here, cot_all, sems):
    moves = [pltpu.make_async_copy(cot, cot_here, sems.at[0])]
    for side, (out, first) in enumerate(((upward, PLANES - HALO), (downward, 0))):
        for ci in range(4):
            moves.append(
                pltpu.make_async_copy(
                    vol.at[ci, first : first + HALO],
                    out.at[ci * HALO : ci * HALO + HALO],
                    sems.at[1 + side * 4 + ci],
                )
            )
    for move in moves:
        move.start()
    moves[0].wait()
    cot_all[0:512, :] = cot_here[...].astype(F32)
    for out, plane in ((upward, 3), (downward, 0)):
        for high in range(4):
            block, lane0 = 20 + high // 2 * 4, high % 2 * 128
            tile = cot_all[pl.ds(plane * 4 + high, 32, stride=16), :]
            out[block : block + 4, :, lane0 : lane0 + 128] = tile.reshape(4, 8, 128).astype(BF16)
    for move in moves[1:]:
        move.wait()


def column(row, height):
    count = row.shape[1]
    at = lax.broadcasted_iota(jnp.int32, (height, count), 0) % count
    lane = lax.broadcasted_iota(jnp.int32, (height, count), 1)
    return jnp.sum(jnp.where(at == lane, row, 0.0), axis=1, keepdims=True)


def prepare(first, bias_one, second, bias_two, w1, b1, w2, b2, w3, wide_one, wide_two, bands):
    b1[...] = column(bias_one[...], 64)
    b2[...] = column(bias_two[...], 32)
    wide_one[...] = jnp.zeros((112, 128), F32)
    wide_one[0:108, 0:16] = first[...].astype(F32)
    bands[...] = jnp.zeros((384, 128), F32)
    for at in range(6):
        total = jnp.zeros((36, 128), F32)
        for kd in range(3):
            j = at - kd
            if 0 <= j < 4:
                piece = wide_one[kd * 36 : kd * 36 + 36, :]
                total = total + (pltpu.roll(piece, 16 * j, 1) if j else piece)
        bands[pl.ds(at // 4 * 144 + at % 4, 36, stride=4), :] = total
    w1[...] = bands[...].T[0:64, 0:288].astype(BF16)
    wide_two[...] = jnp.zeros((512, 128), F32)
    wide_two[0:432, 0:32] = second[...].astype(F32)
    w2[...] = wide_two[...].T[0:32, 0:432].astype(BF16)
    for quad in range(7):
        total = wide_two[(26 - quad * 4) * 16 : (26 - quad * 4) * 16 + 16, :]
        for k in range(1, 4):
            tap = 26 - quad * 4 - k
            if tap >= 0:
                total = total + pltpu.roll(wide_two[tap * 16 : tap * 16 + 16, :], 32 * k, 1)
        w3[:, quad * 128 : quad * 128 + 128] = total.astype(BF16)


def unpack(scale_one, scale_two, core, mine, other, grad_one, shift_one, grad_two, shift_two, whole):
    low = core[0] == 0
    whole[0:72, :] = jnp.where(low, mine[...], other[...])
    whole[72:144, :] = jnp.where(low, other[...], mine[...])
    for group in range(4):
        rows = whole[0:112, :] * scale_two
        if group:
            rows = pltpu.roll(rows, 128 - 32 * group, 1)
        count = 7 if group < 3 else 6
        for tap in range(count):
            grad_two[group * 7 + tap] = rows[tap * 16 : tap * 16 + 16, 0:32]
    for kd in range(3):
        for tap in range(9):
            at, lane0 = (tap, 0) if tap < 6 else (tap - 6, 48)
            piece = whole[112 + at * 4 : 116 + at * 4, :] * scale_one
            lane0 += 16 * kd
            if lane0:
                piece = pltpu.roll(piece, 128 - lane0, 1)
            grad_one[kd * 9 + tap] = piece[:, 0:16]
    row = whole[136:144, :]
    shift_two[...] = row[0:1, 0:32] * scale_two
    shift_one[...] = pltpu.roll(row, 96, 1)[0:1, 0:16] * scale_one


def in_vmem(count):
    return [pl.BlockSpec(memory_space=pltpu.VMEM)] * count


def run_layers(flags, *arrays):
    return pl.pallas_call(
        layers,
        out_shape=(
            jax.ShapeDtypeStruct((512, 128), BF16),
            jax.ShapeDtypeStruct((256, 128), BF16),
            jax.ShapeDtypeStruct((144, 128), F32),
        ),
        in_specs=[pl.BlockSpec(memory_space=pltpu.SMEM)] + in_vmem(len(arrays)),
        out_specs=tuple(in_vmem(3)),
        scratch_shapes=[
            pltpu.VMEM((4, 648, 128), F32),
            pltpu.VMEM((720, 2048), BF16),
            pltpu.VMEM((1152, 512), BF16),
            pltpu.VMEM((1728, 512), BF16),
            pltpu.VMEM((128, 2048), F32),
            pltpu.VMEM((128, 2048), BF16),
            pltpu.VMEM((528, 128), F32),
            pltpu.VMEM((528, 128), F32),
            pltpu.VMEM((272, 128), F32),
            pltpu.VMEM((304, 128), F32),
            pltpu.VMEM((48, 128), F32),
        ],
        compiler_params=pltpu.CompilerParams(vmem_limit_bytes=24 << 20),
        name="layers",
    )(flags, *arrays)


def run_edges(sample, target):
    return pl.pallas_call(
        edges,
        out_shape=(jax.ShapeDtypeStruct((28, 8, 256), BF16),) * 2,
        in_specs=[pl.BlockSpec(memory_space=pl.ANY)] * 2,
        out_specs=tuple(in_vmem(2)),
        scratch_shapes=[
            pltpu.VMEM((512, 128), BF16),
            pltpu.VMEM((528, 128), F32),
            pltpu.SemaphoreType.DMA((9,)),
        ],
        compiler_params=pltpu.CompilerParams(vmem_limit_bytes=4 << 20),
        name="edges",
    )(sample, target)


def run_prepare(*filters):
    return pl.pallas_call(
        prepare,
        out_shape=(
            jax.ShapeDtypeStruct((64, 288), BF16),
            jax.ShapeDtypeStruct((64, 1), F32),
            jax.ShapeDtypeStruct((32, 432), BF16),
            jax.ShapeDtypeStruct((32, 1), F32),
            jax.ShapeDtypeStruct((16, 896), BF16),
        ),
        in_specs=in_vmem(4),
        out_specs=tuple(in_vmem(5)),
        scratch_shapes=[
            pltpu.VMEM((112, 128), F32),
            pltpu.VMEM((512, 128), F32),
            pltpu.VMEM((384, 128), F32),
        ],
        compiler_params=pltpu.CompilerParams(vmem_limit_bytes=4 << 20),
        name="prepare",
    )(*filters)


def run_unpack(scales, core_index, mine, other):
    return pl.pallas_call(
        functools.partial(unpack, *scales),
        out_shape=(
            jax.ShapeDtypeStruct((27, 4, 16), F32),
            jax.ShapeDtypeStruct((1, 16), F32),
            jax.ShapeDtypeStruct((27, 16, 32), F32),
            jax.ShapeDtypeStruct((1, 32), F32),
        ),
        in_specs=[pl.BlockSpec(memory_space=pltpu.SMEM)] + in_vmem(2),
        out_specs=tuple(in_vmem(4)),
        scratch_shapes=[pltpu.VMEM((144, 128), F32)],
        compiler_params=pltpu.CompilerParams(vmem_limit_bytes=4 << 20),
        name="unpack",
    )(core_index, mine, other)


def device_exchanges():
    def place(index):
        dp, space = divmod(index, 16)
        return [dp & 1, (dp >> 1) & 3, space & 3, (dp >> 3) * 4 + (space >> 2)]

    def index_of(core, x, y, z):
        return ((z >> 2) * 8 + x * 2 + core) * 16 + (z & 3) * 4 + y

    def pairing(*masks):
        pairs = []
        for index in range(256):
            spot = [at ^ mask for at, mask in zip(place(index), masks)]
            pairs.append((index, index_of(*spot)))
        return pairs

    fours = (
        (pairing(0, 0, 1, 0), pairing(0, 1, 0, 0), pairing(0, 1, 1, 0)),
        (pairing(0, 0, 3, 0), pairing(0, 3, 0, 0), pairing(0, 3, 3, 0)),
        (pairing(0, 0, 0, 1), pairing(0, 0, 0, 2), pairing(0, 0, 0, 3)),
    )
    return pairing(1, 0, 0, 0), fours, pairing(0, 0, 0, 7)


def add_up(grads, core_index):
    axes = ("dp", "space")
    core, fours, last = device_exchanges()
    low = core_index == 0
    top, bottom = grads[:72], grads[72:]
    mine = jnp.where(low, top, bottom) + lax.ppermute(jnp.where(low, bottom, top), axes, core)
    for first, second, third in fours:
        one, two, three = (lax.ppermute(mine, axes, pairs) for pairs in (first, second, third))
        mine = lax.optimization_barrier((mine + one) + (two + three))
    mine = mine + lax.ppermute(mine, axes, last)
    return mine, lax.ppermute(mine, axes, core)


def as_rows(first_filters, first_biases, second_filters, second_biases):
    return (
        first_filters.transpose(2, 3, 4, 1, 0).reshape(108, 16),
        first_biases[None],
        second_filters.transpose(2, 3, 4, 1, 0).reshape(432, 32),
        second_biases[None],
    )


def shards(volume, first_filters, first_biases, second_filters, second_biases, cotangent):
    sample, target = volume[0], cotangent[0]
    slabs = lax.axis_size("space")
    here = lax.axis_index("space")
    forward = [(i, i + 1) for i in range(slabs - 1)]
    backward = [(i + 1, i) for i in range(slabs - 1)]
    target = target.reshape(512, 128)
    upward, downward = run_edges(sample, target)
    below = lax.ppermute(upward, "space", forward)
    above = lax.ppermute(downward, "space", backward)
    matrices = run_prepare(*as_rows(first_filters, first_biases, second_filters, second_biases))
    flags = jnp.stack([here > 0, here < slabs - 1]).astype(F32)
    act, pooled_grad, grads = run_layers(flags, sample, below, above, target, *matrices)
    core_index = lax.axis_index("dp") % 2
    mine, other = add_up(grads, core_index)
    count_one = (
        lax.axis_size("dp") * slabs * PLANES * sample.shape[2] * sample.shape[3]
    )
    scales = (1.0 / math.sqrt(count_one), 1.0 / math.sqrt(count_one / 8))
    grad_one, shift_one, grad_two, shift_two = run_unpack(scales, core_index[None], mine, other)
    return (
        act.reshape(1, 32, 4, 4, 128),
        pooled_grad.reshape(1, 16, 4, 4, 128),
        grad_one.reshape(3, 3, 3, 4, 16).transpose(4, 3, 0, 1, 2),
        shift_one[0],
        grad_two.reshape(3, 3, 3, 16, 32).transpose(4, 3, 0, 1, 2),
        shift_two[0],
    )


def solution(mesh):
    slab = P("dp", None, "space", None, None)
    return jax.shard_map(
        shards,
        mesh=mesh,
        in_specs=(slab, P(), P(), P(), P(), slab),
        out_specs=(slab, slab, P(), P(), P(), P()),
        check_vma=False,
    )
```

```python
import functools
import math

import jax
import jax.numpy as jnp
from jax import lax
from jax.experimental import pallas as pl
from jax.experimental.pallas import tpu as pltpu
from jax.sharding import PartitionSpec as P

F32 = jnp.float32
BF16 = jnp.bfloat16
HALO = 5
PLANES = 8
LEAK = 0.3


def lanes_dot(left, right):
    return lax.dot_general(left, right, (((1,), (1,)), ((), ())), preferred_element_type=F32)


def plain_dot(left, right):
    return jnp.dot(left, right, preferred_element_type=F32)


def both_shifts(values):
    lane = lax.broadcasted_iota(jnp.int32, values.shape, 1)
    before = jnp.where(lane == 0, 0.0, pltpu.roll(values, 1, 1))
    after = jnp.where(lane == 127, 0.0, pltpu.roll(values, 127, 1))
    return before.astype(BF16), values.astype(BF16), after.astype(BF16)


def layers(
    flags, vol, below, above, cot, w1, b1, w2, b2, w3,
    act_out, pooled_grad_out, grads,
    act, pooled_grad, sems, split, x1, x2, x3, slope, delta_one, cot_all, act_all, grad_all, band, thin,
):
    row = lax.broadcasted_iota(jnp.int32, (256, 512), 0)
    col = lax.broadcasted_iota(jnp.int32, (256, 512), 1)
    kind = col // 128
    offset = jnp.where(kind == 0, 0, jnp.where(kind == 1, 1, jnp.where(kind == 2, -1, 2)))
    pick = (row == 2 * (col % 128) + offset).astype(F32).astype(BF16)
    for ci in range(4):
        planes = jnp.concatenate(
            [
                below[ci * HALO : ci * HALO + HALO].astype(F32).reshape(40, 256),
                vol[ci].astype(F32).reshape(64, 256),
                above[ci * HALO : ci * HALO + HALO].astype(F32).reshape(40, 256),
                jnp.zeros((16, 256), F32),
            ],
            axis=0,
        )
        parts = plain_dot(planes.astype(BF16), pick)
        for group in range(5):
            for kind_n in range(4):
                split[kind_n, (group * 4 + ci) * 32 : (group * 4 + ci + 1) * 32, :] = parts[
                    group * 32 : group * 32 + 32, kind_n * 128 : kind_n * 128 + 128
                ]
    homes = {0: ((0, 1), (1, 0)), 1: ((0, 2), (1, 1)), 2: ((0, 0),), 3: ((1, 2),)}
    for group in range(5):
        base = group * 144
        x1[base : base + 48, 0:256] = jnp.zeros((48, 256), BF16)
        x1[base + 96 : base + 144, 1792:2048] = jnp.zeros((48, 256), BF16)
    for height in range(8):
        for kind_n in range(4):
            tile = split[kind_n, pl.ds(height, 80, stride=8), :].astype(BF16)
            for kh in range(3):
                out_h = height - kh + 1
                if not 0 <= out_h < 8:
                    continue
                for parity, kw in homes[kind_n]:
                    lane0 = out_h * 256 + parity * 128
                    for group in range(5):
                        row0 = group * 144 + (kh * 3 + kw) * 16
                        x1[row0 : row0 + 16, lane0 : lane0 + 128] = tile[
                            group * 16 : group * 16 + 16
                        ]
    for plane in range(8):
        base = plane * 144
        x2[base : base + 48, 0:128] = jnp.zeros((48, 128), BF16)
        x2[base + 96 : base + 144, 384:512] = jnp.zeros((48, 128), BF16)
    weights_one = w1[...]
    bias_one = b1[...]
    for high in range(4):
        everything = plain_dot(weights_one, x1[:, high * 512 : high * 512 + 512])
        for group in range(4):
            linear = everything[group * 64 : group * 64 + 64]
            linear = linear + bias_one
            positive = linear > 0
            if group in (1, 2):
                slope[(group - 1) * 64 : group * 64, high * 512 : high * 512 + 512] = jnp.where(
                    positive, 0.125, 0.125 * LEAK
                )
            leaky = jnp.where(positive, linear, LEAK * linear)
            for pair in range(2):
                both = leaky[pair * 32 : pair * 32 + 16] + leaky[pair * 32 + 16 : pair * 32 + 32]
                mean = (
                    (both[:, 0:128] + both[:, 128:256]) + (both[:, 256:384] + both[:, 384:512])
                ) * 0.125
                plane = group * 2 + pair
                if plane < 2:
                    mean = mean * flags[0]
                if plane >= 6:
                    mean = mean * flags[1]
                for kw, moved in enumerate(both_shifts(mean)):
                    for kh in range(3):
                        out_h = high - kh + 1
                        if 0 <= out_h < 4:
                            row0 = plane * 144 + (kh * 3 + kw) * 16
                            x2[row0 : row0 + 16, out_h * 128 : out_h * 128 + 128] = moved
    cot_all[0:512, :] = cot[...].astype(F32)
    for plane in range(6):
        base = plane * 288
        x3[base : base + 96, 0:128] = jnp.zeros((96, 128), BF16)
        x3[base + 192 : base + 288, 384:512] = jnp.zeros((96, 128), BF16)
    weights_two = w2[...]
    bias_two = b2[...]
    everything = plain_dot(weights_two, x2[...])
    for plane in range(6):
        linear = everything[plane * 32 : plane * 32 + 32] + bias_two
        positive = linear > 0
        factor = jnp.where(positive, 1.0, LEAK)
        leaky = jnp.where(positive, linear, LEAK * linear)
        for high in range(4):
            lanes = slice(high * 128, high * 128 + 128)
            if plane in (0, 5):
                outer = below if plane == 0 else above
                block, lane0 = 20 + high // 2 * 4, high % 2 * 128
                target = outer[block : block + 4, :, lane0 : lane0 + 128].astype(F32)
                target = target.reshape(32, 128)
            else:
                at = (plane - 1) * 4 + high
                target = cot_all[pl.ds(at, 32, stride=16), :]
                act_all[pl.ds(at, 32, stride=16), :] = leaky[:, lanes]
            delta = target * factor[:, lanes]
            for kw, moved in enumerate(both_shifts(delta)):
                for kh in range(3):
                    out_h = high - kh + 1
                    if 0 <= out_h < 4:
                        row0 = plane * 288 + (kh * 3 + kw) * 32
                        x3[row0 : row0 + 32, out_h * 128 : out_h * 128 + 128] = moved
    act[...] = act_all[0:512, :].astype(BF16)
    act_move = pltpu.make_async_copy(act, act_out, sems.at[0])
    act_move.start()
    everything = plain_dot(w3[...], x3[...])
    for plane in range(4):
        total = everything[plane * 16 : plane * 16 + 16]
        for high in range(4):
            tile = total[:, high * 128 : high * 128 + 128].astype(BF16).astype(F32)
            grad_all[pl.ds(plane * 4 + high, 16, stride=16), :] = tile
            for row0 in (plane * 32, plane * 32 + 16):
                for part in range(4):
                    lane0 = high * 512 + part * 128
                    delta_one[row0 : row0 + 16, lane0 : lane0 + 128] = (
                        tile * slope[row0 : row0 + 16, lane0 : lane0 + 128]
                    ).astype(BF16)
    pooled_grad[...] = grad_all[0:256, :].astype(BF16)
    pooled_grad_move = pltpu.make_async_copy(pooled_grad, pooled_grad_out, sems.at[1])
    pooled_grad_move.start()
    second = jnp.zeros((432, 128), F32)
    shift_two = jnp.zeros((16, 128), F32)
    for plane in range(4):
        delta = jnp.concatenate(
            [x3[(plane + 1) * 288 + 128 : (plane + 1) * 288 + 160, :], jnp.zeros((96, 512), BF16)],
            axis=0,
        )
        second = second + lanes_dot(x2[(plane + 1) * 144 : (plane + 1) * 144 + 432, :], delta)
        shift_two = shift_two + lanes_dot(jnp.ones((16, 512), BF16), delta)
    three = (
        second[0:112] + pltpu.roll(second[112:224], 32, 1) + pltpu.roll(second[224:336], 64, 1)
    )
    grads[0:96, :] = three[0:96] + pltpu.roll(second[336:432], 96, 1)
    grads[96:112, :] = three[96:112]
    first = jnp.zeros((288, 128), F32)
    shift_one = jnp.zeros((16, 128), F32)
    for group in (1, 2):
        delta = jnp.concatenate(
            [delta_one[(group - 1) * 64 : group * 64, :], jnp.zeros((64, 2048), BF16)], axis=0
        )
        first = first + lanes_dot(x1[group * 144 : group * 144 + 288, :], delta)
        shift_one = shift_one + lanes_dot(jnp.ones((16, 2048), BF16), delta)
    band[0:288, :] = first
    lane36 = lax.broadcasted_iota(jnp.int32, (36, 128), 1)
    packed = jnp.zeros((36, 128), F32)
    for kd in range(3):
        total = jnp.zeros((36, 128), F32)
        for plane in range(4):
            at = (plane + kd) // 4 * 144 + (plane + kd) % 4
            piece = band[pl.ds(at, 36, stride=4), :]
            lane0 = (128 + 16 * (kd - plane)) % 128
            total = total + (pltpu.roll(piece, lane0, 1) if lane0 else piece)
        packed = packed + jnp.where((lane36 >= 16 * kd) & (lane36 < 16 * kd + 16), total, 0.0)
    thin[...] = jnp.zeros((48, 128), F32)
    thin[0:36, :] = packed
    grads[112:136, :] = thin[0:24, :] + pltpu.roll(thin[24:48, :], 48, 1)
    lane = lax.broadcasted_iota(jnp.int32, (8, 128), 1)
    ones = shift_one[0:8]
    ones = (
        ones + pltpu.roll(ones, 112, 1) + pltpu.roll(ones, 96, 1) + pltpu.roll(ones, 80, 1)
    )
    ones = jnp.where((lane >= 32) & (lane < 48), pltpu.roll(ones, 32, 1), 0.0)
    grads[136:144, :] = jnp.where(lane < 32, shift_two[0:8], ones)
    act_move.wait()
    pooled_grad_move.wait()


def edges(vol, cot, upward, downward, cot_here, cot_all, sems):
    moves = [pltpu.make_async_copy(cot, cot_here, sems.at[0])]
    for side, (out, first) in enumerate(((upward, PLANES - HALO), (downward, 0))):
        for ci in range(4):
            moves.append(
                pltpu.make_async_copy(
                    vol.at[ci, first : first + HALO],
                    out.at[ci * HALO : ci * HALO + HALO],
                    sems.at[1 + side * 4 + ci],
                )
            )
    for move in moves:
        move.start()
    moves[0].wait()
    cot_all[0:512, :] = cot_here[...].astype(F32)
    for out, plane in ((upward, 3), (downward, 0)):
        for high in range(4):
            block, lane0 = 20 + high // 2 * 4, high % 2 * 128
            tile = cot_all[pl.ds(plane * 4 + high, 32, stride=16), :]
            out[block : block + 4, :, lane0 : lane0 + 128] = tile.reshape(4, 8, 128).astype(BF16)
    for move in moves[1:]:
        move.wait()


def column(row, height):
    count = row.shape[1]
    at = lax.broadcasted_iota(jnp.int32, (height, count), 0) % count
    lane = lax.broadcasted_iota(jnp.int32, (height, count), 1)
    return jnp.sum(jnp.where(at == lane, row, 0.0), axis=1, keepdims=True)


def prepare(first, bias_one, second, bias_two, w1, b1, w2, b2, w3, wide_one, wide_two, bands):
    b1[...] = column(bias_one[...], 64)
    b2[...] = column(bias_two[...], 32)
    wide_one[...] = jnp.zeros((112, 128), F32)
    wide_one[0:108, 0:16] = first[...].astype(F32)
    bands[...] = jnp.zeros((384, 128), F32)
    for at in range(6):
        total = jnp.zeros((36, 128), F32)
        for kd in range(3):
            j = at - kd
            if 0 <= j < 4:
                piece = wide_one[kd * 36 : kd * 36 + 36, :]
                total = total + (pltpu.roll(piece, 16 * j, 1) if j else piece)
        bands[pl.ds(at // 4 * 144 + at % 4, 36, stride=4), :] = total
    base = jnp.concatenate([bands[...].T[0:64], jnp.zeros((64, 384), F32)], axis=1)
    for group in range(4):
        moved = pltpu.roll(base, group * 144, 1) if group else base
        w1[group * 64 : group * 64 + 64, :] = moved[:, 0:720].astype(BF16)
    wide_two[...] = jnp.zeros((512, 128), F32)
    wide_two[0:432, 0:32] = second[...].astype(F32)
    base = jnp.concatenate([wide_two[...].T[0:32], jnp.zeros((32, 640), F32)], axis=1)
    for plane in range(6):
        moved = pltpu.roll(base, plane * 144, 1) if plane else base
        w2[plane * 32 : plane * 32 + 32, :] = moved.astype(BF16)
    quads = []
    for quad in range(7):
        total = wide_two[(26 - quad * 4) * 16 : (26 - quad * 4) * 16 + 16, :]
        for k in range(1, 4):
            tap = 26 - quad * 4 - k
            if tap >= 0:
                total = total + pltpu.roll(wide_two[tap * 16 : tap * 16 + 16, :], 32 * k, 1)
        quads.append(total)
    base = jnp.concatenate(quads + [jnp.zeros((16, 896), F32)], axis=1)
    for plane in range(4):
        moved = pltpu.roll(base, plane * 288, 1) if plane else base
        w3[plane * 16 : plane * 16 + 16, :] = moved[:, 0:1728].astype(BF16)


def unpack(scale_one, scale_two, core, mine, other, grad_one, shift_one, grad_two, shift_two, whole):
    low = core[0] == 0
    whole[0:72, :] = jnp.where(low, mine[...], other[...])
    whole[72:144, :] = jnp.where(low, other[...], mine[...])
    for group in range(4):
        rows = whole[0:112, :] * scale_two
        if group:
            rows = pltpu.roll(rows, 128 - 32 * group, 1)
        count = 7 if group < 3 else 6
        for tap in range(count):
            grad_two[group * 7 + tap] = rows[tap * 16 : tap * 16 + 16, 0:32]
    for kd in range(3):
        for tap in range(9):
            at, lane0 = (tap, 0) if tap < 6 else (tap - 6, 48)
            piece = whole[112 + at * 4 : 116 + at * 4, :] * scale_one
            lane0 += 16 * kd
            if lane0:
                piece = pltpu.roll(piece, 128 - lane0, 1)
            grad_one[kd * 9 + tap] = piece[:, 0:16]
    row = whole[136:144, :]
    shift_two[...] = row[0:1, 0:32] * scale_two
    shift_one[...] = pltpu.roll(row, 96, 1)[0:1, 0:16] * scale_one


def in_vmem(count):
    return [pl.BlockSpec(memory_space=pltpu.VMEM)] * count


def run_layers(flags, *arrays):
    return pl.pallas_call(
        layers,
        out_shape=(
            jax.ShapeDtypeStruct((512, 128), BF16),
            jax.ShapeDtypeStruct((256, 128), BF16),
            jax.ShapeDtypeStruct((144, 128), F32),
        ),
        in_specs=[pl.BlockSpec(memory_space=pltpu.SMEM)] + in_vmem(len(arrays)),
        out_specs=(
            pl.BlockSpec(memory_space=pl.ANY),
            pl.BlockSpec(memory_space=pl.ANY),
            pl.BlockSpec(memory_space=pltpu.VMEM),
        ),
        scratch_shapes=[
            pltpu.VMEM((512, 128), BF16),
            pltpu.VMEM((256, 128), BF16),
            pltpu.SemaphoreType.DMA((2,)),
            pltpu.VMEM((4, 648, 128), F32),
            pltpu.VMEM((720, 2048), BF16),
            pltpu.VMEM((1152, 512), BF16),
            pltpu.VMEM((1728, 512), BF16),
            pltpu.VMEM((128, 2048), F32),
            pltpu.VMEM((128, 2048), BF16),
            pltpu.VMEM((528, 128), F32),
            pltpu.VMEM((528, 128), F32),
            pltpu.VMEM((272, 128), F32),
            pltpu.VMEM((304, 128), F32),
            pltpu.VMEM((48, 128), F32),
        ],
        compiler_params=pltpu.CompilerParams(vmem_limit_bytes=24 << 20),
        name="layers",
    )(flags, *arrays)


def run_edges(sample, target):
    return pl.pallas_call(
        edges,
        out_shape=(jax.ShapeDtypeStruct((28, 8, 256), BF16),) * 2,
        in_specs=[pl.BlockSpec(memory_space=pltpu.HBM)] * 2,
        out_specs=tuple(in_vmem(2)),
        scratch_shapes=[
            pltpu.VMEM((512, 128), BF16),
            pltpu.VMEM((528, 128), F32),
            pltpu.SemaphoreType.DMA((9,)),
        ],
        compiler_params=pltpu.CompilerParams(vmem_limit_bytes=4 << 20),
        name="edges",
    )(
        pltpu.with_memory_space_constraint(sample, pltpu.HBM),
        pltpu.with_memory_space_constraint(target, pltpu.HBM),
    )


def run_prepare(*filters):
    return pl.pallas_call(
        prepare,
        out_shape=(
            jax.ShapeDtypeStruct((256, 720), BF16),
            jax.ShapeDtypeStruct((64, 1), F32),
            jax.ShapeDtypeStruct((192, 1152), BF16),
            jax.ShapeDtypeStruct((32, 1), F32),
            jax.ShapeDtypeStruct((64, 1728), BF16),
        ),
        in_specs=in_vmem(4),
        out_specs=tuple(in_vmem(5)),
        scratch_shapes=[
            pltpu.VMEM((112, 128), F32),
            pltpu.VMEM((512, 128), F32),
            pltpu.VMEM((384, 128), F32),
        ],
        compiler_params=pltpu.CompilerParams(vmem_limit_bytes=4 << 20),
        name="prepare",
    )(*filters)


def run_unpack(scales, core_index, mine, other):
    return pl.pallas_call(
        functools.partial(unpack, *scales),
        out_shape=(
            jax.ShapeDtypeStruct((27, 4, 16), F32),
            jax.ShapeDtypeStruct((1, 16), F32),
            jax.ShapeDtypeStruct((27, 16, 32), F32),
            jax.ShapeDtypeStruct((1, 32), F32),
        ),
        in_specs=[pl.BlockSpec(memory_space=pltpu.SMEM)] + in_vmem(2),
        out_specs=tuple(in_vmem(4)),
        scratch_shapes=[pltpu.VMEM((144, 128), F32)],
        compiler_params=pltpu.CompilerParams(vmem_limit_bytes=4 << 20),
        name="unpack",
    )(core_index, mine, other)


def device_exchanges():
    def place(index):
        dp, space = divmod(index, 16)
        return [dp & 1, (dp >> 1) & 3, space & 3, (dp >> 3) * 4 + (space >> 2)]

    def index_of(core, x, y, z):
        return ((z >> 2) * 8 + x * 2 + core) * 16 + (z & 3) * 4 + y

    def pairing(*masks):
        pairs = []
        for index in range(256):
            spot = [at ^ mask for at, mask in zip(place(index), masks)]
            pairs.append((index, index_of(*spot)))
        return pairs

    fours = (
        (pairing(0, 0, 1, 0), pairing(0, 1, 0, 0), pairing(0, 1, 1, 0)),
        (pairing(0, 0, 3, 0), pairing(0, 3, 0, 0), pairing(0, 3, 3, 0)),
        (pairing(0, 0, 0, 1), pairing(0, 0, 0, 2), pairing(0, 0, 0, 3)),
    )
    return pairing(1, 0, 0, 0), fours, pairing(0, 0, 0, 7)


def add_up(grads, core_index):
    axes = ("dp", "space")
    core, fours, last = device_exchanges()
    low = core_index == 0
    top, bottom = grads[:72], grads[72:]
    mine = jnp.where(low, top, bottom) + lax.ppermute(jnp.where(low, bottom, top), axes, core)
    for first, second, third in fours:
        one, two, three = (lax.ppermute(mine, axes, pairs) for pairs in (first, second, third))
        mine = lax.optimization_barrier((mine + one) + (two + three))
    mine = mine + lax.ppermute(mine, axes, last)
    return mine, lax.ppermute(mine, axes, core)


def as_rows(first_filters, first_biases, second_filters, second_biases):
    return (
        first_filters.transpose(2, 3, 4, 1, 0).reshape(108, 16),
        first_biases[None],
        second_filters.transpose(2, 3, 4, 1, 0).reshape(432, 32),
        second_biases[None],
    )


def shards(volume, first_filters, first_biases, second_filters, second_biases, cotangent):
    sample, target = volume[0], cotangent[0]
    slabs = lax.axis_size("space")
    here = lax.axis_index("space")
    forward = [(i, i + 1) for i in range(slabs - 1)]
    backward = [(i + 1, i) for i in range(slabs - 1)]
    target = target.reshape(512, 128)
    upward, downward = run_edges(sample, target)
    below = lax.ppermute(upward, "space", forward)
    above = lax.ppermute(downward, "space", backward)
    matrices = run_prepare(*as_rows(first_filters, first_biases, second_filters, second_biases))
    flags = jnp.stack([here > 0, here < slabs - 1]).astype(F32)
    act, pooled_grad, grads = run_layers(flags, sample, below, above, target, *matrices)
    core_index = lax.axis_index("dp") % 2
    mine, other = add_up(grads, core_index)
    count_one = (
        lax.axis_size("dp") * slabs * PLANES * sample.shape[2] * sample.shape[3]
    )
    scales = (1.0 / math.sqrt(count_one), 1.0 / math.sqrt(count_one / 8))
    grad_one, shift_one, grad_two, shift_two = run_unpack(scales, core_index[None], mine, other)
    return (
        act.reshape(1, 32, 4, 4, 128),
        pooled_grad.reshape(1, 16, 4, 4, 128),
        grad_one.reshape(3, 3, 3, 4, 16).transpose(4, 3, 0, 1, 2),
        shift_one[0],
        grad_two.reshape(3, 3, 3, 16, 32).transpose(4, 3, 0, 1, 2),
        shift_two[0],
    )


def solution(mesh):
    slab = P("dp", None, "space", None, None)
    return jax.shard_map(
        shards,
        mesh=mesh,
        in_specs=(slab, P(), P(), P(), P(), slab),
        out_specs=(slab, slab, P(), P(), P(), P()),
        check_vma=False,
    )
```

```python
import functools
import math

import jax
import jax.numpy as jnp
from jax import lax
from jax.experimental import pallas as pl
from jax.experimental.pallas import tpu as pltpu
from jax.sharding import PartitionSpec as P

F32 = jnp.float32
BF16 = jnp.bfloat16
HALO = 5
PLANES = 8
LEAK = 0.3


def lanes_dot(left, right):
    return lax.dot_general(left, right, (((1,), (1,)), ((), ())), preferred_element_type=F32)


def plain_dot(left, right):
    return jnp.dot(left, right, preferred_element_type=F32)


def both_shifts(values):
    lane = lax.broadcasted_iota(jnp.int32, values.shape, 1)
    before = jnp.where(lane == 0, 0.0, pltpu.roll(values, 1, 1))
    after = jnp.where(lane == 127, 0.0, pltpu.roll(values, 127, 1))
    return before.astype(BF16), values.astype(BF16), after.astype(BF16)


def layers(
    flags, vol, below, above, cot, w1, b1, w2, b2, w3,
    act_out, pooled_grad_out, grads,
    act, pooled_grad, sems, split, x1, x2, x3, slope, delta_one, cot_all, act_all, grad_all, band, thin,
):
    row = lax.broadcasted_iota(jnp.int32, (256, 512), 0)
    col = lax.broadcasted_iota(jnp.int32, (256, 512), 1)
    kind = col // 128
    offset = jnp.where(kind == 0, 0, jnp.where(kind == 1, 1, jnp.where(kind == 2, -1, 2)))
    pick = (row == 2 * (col % 128) + offset).astype(F32).astype(BF16)
    for ci in range(4):
        planes = jnp.concatenate(
            [
                below[ci * HALO : ci * HALO + HALO].astype(F32).reshape(40, 256),
                vol[ci].astype(F32).reshape(64, 256),
                above[ci * HALO : ci * HALO + HALO].astype(F32).reshape(40, 256),
                jnp.zeros((16, 256), F32),
            ],
            axis=0,
        )
        parts = plain_dot(planes.astype(BF16), pick)
        for group in range(5):
            for kind_n in range(4):
                split[kind_n, (group * 4 + ci) * 32 : (group * 4 + ci + 1) * 32, :] = parts[
                    group * 32 : group * 32 + 32, kind_n * 128 : kind_n * 128 + 128
                ]
    homes = {0: ((0, 1), (1, 0)), 1: ((0, 2), (1, 1)), 2: ((0, 0),), 3: ((1, 2),)}
    for group in range(5):
        base = group * 144
        x1[base : base + 48, 0:256] = jnp.zeros((48, 256), BF16)
        x1[base + 96 : base + 144, 1792:2048] = jnp.zeros((48, 256), BF16)
    for height in range(8):
        for kind_n in range(4):
            tile = split[kind_n, pl.ds(height, 80, stride=8), :].astype(BF16)
            for kh in range(3):
                out_h = height - kh + 1
                if not 0 <= out_h < 8:
                    continue
                for parity, kw in homes[kind_n]:
                    lane0 = out_h * 256 + parity * 128
                    for group in range(5):
                        row0 = group * 144 + (kh * 3 + kw) * 16
                        x1[row0 : row0 + 16, lane0 : lane0 + 128] = tile[
                            group * 16 : group * 16 + 16
                        ]
    for plane in range(8):
        base = plane * 144
        x2[base : base + 48, 0:128] = jnp.zeros((48, 128), BF16)
        x2[base + 96 : base + 144, 384:512] = jnp.zeros((48, 128), BF16)
    weights_one = w1[...]
    bias_one = b1[...]
    for high in range(4):
        everything = plain_dot(weights_one, x1[:, high * 512 : high * 512 + 512])
        for group in range(4):
            linear = everything[group * 64 : group * 64 + 64]
            linear = linear + bias_one
            positive = linear > 0
            if group in (1, 2):
                slope[(group - 1) * 64 : group * 64, high * 512 : high * 512 + 512] = jnp.where(
                    positive, 0.125, 0.125 * LEAK
                )
            leaky = jnp.where(positive, linear, LEAK * linear)
            for pair in range(2):
                both = leaky[pair * 32 : pair * 32 + 16] + leaky[pair * 32 + 16 : pair * 32 + 32]
                mean = (
                    (both[:, 0:128] + both[:, 128:256]) + (both[:, 256:384] + both[:, 384:512])
                ) * 0.125
                plane = group * 2 + pair
                if plane < 2:
                    mean = mean * flags[0]
                if plane >= 6:
                    mean = mean * flags[1]
                for kw, moved in enumerate(both_shifts(mean)):
                    for kh in range(3):
                        out_h = high - kh + 1
                        if 0 <= out_h < 4:
                            row0 = plane * 144 + (kh * 3 + kw) * 16
                            x2[row0 : row0 + 16, out_h * 128 : out_h * 128 + 128] = moved
    cot_all[0:512, :] = cot[...].astype(F32)
    for plane in range(6):
        base = plane * 288
        x3[base : base + 96, 0:128] = jnp.zeros((96, 128), BF16)
        x3[base + 192 : base + 288, 384:512] = jnp.zeros((96, 128), BF16)
    weights_two = w2[...]
    bias_two = b2[...]
    everything = plain_dot(weights_two, x2[...])
    for plane in range(6):
        linear = everything[plane * 32 : plane * 32 + 32] + bias_two
        positive = linear > 0
        factor = jnp.where(positive, 1.0, LEAK)
        leaky = jnp.where(positive, linear, LEAK * linear)
        for high in range(4):
            lanes = slice(high * 128, high * 128 + 128)
            if plane in (0, 5):
                outer = below if plane == 0 else above
                block, lane0 = 20 + high // 2 * 4, high % 2 * 128
                target = outer[block : block + 4, :, lane0 : lane0 + 128].astype(F32)
                target = target.reshape(32, 128)
            else:
                at = (plane - 1) * 4 + high
                target = cot_all[pl.ds(at, 32, stride=16), :]
                act_all[pl.ds(at, 32, stride=16), :] = leaky[:, lanes]
            delta = target * factor[:, lanes]
            for kw, moved in enumerate(both_shifts(delta)):
                for kh in range(3):
                    out_h = high - kh + 1
                    if 0 <= out_h < 4:
                        row0 = plane * 288 + (kh * 3 + kw) * 32
                        x3[row0 : row0 + 32, out_h * 128 : out_h * 128 + 128] = moved
    act[...] = act_all[0:512, :].astype(BF16)
    act_move = pltpu.make_async_copy(act, act_out, sems.at[0])
    act_move.start()
    everything = plain_dot(w3[...], x3[...])
    for plane in range(4):
        total = everything[plane * 16 : plane * 16 + 16]
        for high in range(4):
            tile = total[:, high * 128 : high * 128 + 128].astype(BF16).astype(F32)
            grad_all[pl.ds(plane * 4 + high, 16, stride=16), :] = tile
            for row0 in (plane * 32, plane * 32 + 16):
                for part in range(4):
                    lane0 = high * 512 + part * 128
                    delta_one[row0 : row0 + 16, lane0 : lane0 + 128] = (
                        tile * slope[row0 : row0 + 16, lane0 : lane0 + 128]
                    ).astype(BF16)
    pooled_grad[...] = grad_all[0:256, :].astype(BF16)
    pooled_grad_move = pltpu.make_async_copy(pooled_grad, pooled_grad_out, sems.at[1])
    pooled_grad_move.start()
    second = jnp.zeros((432, 128), F32)
    shift_two = jnp.zeros((16, 128), F32)
    for plane in range(4):
        delta = jnp.concatenate(
            [x3[(plane + 1) * 288 + 128 : (plane + 1) * 288 + 160, :], jnp.zeros((96, 512), BF16)],
            axis=0,
        )
        second = second + lanes_dot(x2[(plane + 1) * 144 : (plane + 1) * 144 + 432, :], delta)
        shift_two = shift_two + lanes_dot(jnp.ones((16, 512), BF16), delta)
    three = (
        second[0:112] + pltpu.roll(second[112:224], 32, 1) + pltpu.roll(second[224:336], 64, 1)
    )
    grads[0:96, :] = three[0:96] + pltpu.roll(second[336:432], 96, 1)
    grads[96:112, :] = three[96:112]
    delta = delta_one[...]
    band[0:432, :] = lanes_dot(x1[144:576, :], delta)
    shift_one = lanes_dot(jnp.ones((16, 2048), BF16), delta)
    lane36 = lax.broadcasted_iota(jnp.int32, (36, 128), 1)
    packed = jnp.zeros((36, 128), F32)
    for kd in range(3):
        total = jnp.zeros((36, 128), F32)
        for plane in range(8):
            at = (plane + kd) // 4 * 144 + (plane + kd) % 4
            piece = band[pl.ds(at, 36, stride=4), :]
            lane0 = (128 + 16 * (kd - plane)) % 128
            total = total + (pltpu.roll(piece, lane0, 1) if lane0 else piece)
        packed = packed + jnp.where((lane36 >= 16 * kd) & (lane36 < 16 * kd + 16), total, 0.0)
    thin[...] = jnp.zeros((48, 128), F32)
    thin[0:36, :] = packed
    grads[112:136, :] = thin[0:24, :] + pltpu.roll(thin[24:48, :], 48, 1)
    lane = lax.broadcasted_iota(jnp.int32, (8, 128), 1)
    ones = shift_one[0:8]
    for shift in (64, 32, 16):
        ones = ones + pltpu.roll(ones, shift, 1)
    ones = jnp.where((lane >= 32) & (lane < 48), ones, 0.0)
    grads[136:144, :] = jnp.where(lane < 32, shift_two[0:8], ones)
    act_move.wait()
    pooled_grad_move.wait()


def edges(vol, cot, upward, downward, cot_here, cot_all, sems):
    moves = [pltpu.make_async_copy(cot, cot_here, sems.at[0])]
    for side, (out, first) in enumerate(((upward, PLANES - HALO), (downward, 0))):
        for ci in range(4):
            moves.append(
                pltpu.make_async_copy(
                    vol.at[ci, first : first + HALO],
                    out.at[ci * HALO : ci * HALO + HALO],
                    sems.at[1 + side * 4 + ci],
                )
            )
    for move in moves:
        move.start()
    moves[0].wait()
    cot_all[0:512, :] = cot_here[...].astype(F32)
    for out, plane in ((upward, 3), (downward, 0)):
        for high in range(4):
            block, lane0 = 20 + high // 2 * 4, high % 2 * 128
            tile = cot_all[pl.ds(plane * 4 + high, 32, stride=16), :]
            out[block : block + 4, :, lane0 : lane0 + 128] = tile.reshape(4, 8, 128).astype(BF16)
    for move in moves[1:]:
        move.wait()


def column(row, height):
    count = row.shape[1]
    at = lax.broadcasted_iota(jnp.int32, (height, count), 0) % count
    lane = lax.broadcasted_iota(jnp.int32, (height, count), 1)
    return jnp.sum(jnp.where(at == lane, row, 0.0), axis=1, keepdims=True)


def prepare(first, bias_one, second, bias_two, w1, b1, w2, b2, w3, wide_one, wide_two, bands):
    b1[...] = column(bias_one[...], 64)
    b2[...] = column(bias_two[...], 32)
    wide_one[...] = jnp.zeros((112, 128), F32)
    wide_one[0:108, 0:16] = first[...].astype(F32)
    bands[...] = jnp.zeros((384, 128), F32)
    for at in range(6):
        total = jnp.zeros((36, 128), F32)
        for kd in range(3):
            j = at - kd
            if 0 <= j < 4:
                piece = wide_one[kd * 36 : kd * 36 + 36, :]
                total = total + (pltpu.roll(piece, 16 * j, 1) if j else piece)
        bands[pl.ds(at // 4 * 144 + at % 4, 36, stride=4), :] = total
    base = jnp.concatenate([bands[...].T[0:64], jnp.zeros((64, 384), F32)], axis=1)
    for group in range(4):
        moved = pltpu.roll(base, group * 144, 1) if group else base
        w1[group * 64 : group * 64 + 64, :] = moved[:, 0:720].astype(BF16)
    wide_two[...] = jnp.zeros((512, 128), F32)
    wide_two[0:432, 0:32] = second[...].astype(F32)
    base = jnp.concatenate([wide_two[...].T[0:32], jnp.zeros((32, 640), F32)], axis=1)
    for plane in range(6):
        moved = pltpu.roll(base, plane * 144, 1) if plane else base
        w2[plane * 32 : plane * 32 + 32, :] = moved.astype(BF16)
    quads = []
    for quad in range(7):
        total = wide_two[(26 - quad * 4) * 16 : (26 - quad * 4) * 16 + 16, :]
        for k in range(1, 4):
            tap = 26 - quad * 4 - k
            if tap >= 0:
                total = total + pltpu.roll(wide_two[tap * 16 : tap * 16 + 16, :], 32 * k, 1)
        quads.append(total)
    base = jnp.concatenate(quads + [jnp.zeros((16, 896), F32)], axis=1)
    for plane in range(4):
        moved = pltpu.roll(base, plane * 288, 1) if plane else base
        w3[plane * 16 : plane * 16 + 16, :] = moved[:, 0:1728].astype(BF16)


def unpack(scale_one, scale_two, core, mine, other, grad_one, shift_one, grad_two, shift_two, whole):
    low = core[0] == 0
    whole[0:72, :] = jnp.where(low, mine[...], other[...])
    whole[72:144, :] = jnp.where(low, other[...], mine[...])
    for group in range(4):
        rows = whole[0:112, :] * scale_two
        if group:
            rows = pltpu.roll(rows, 128 - 32 * group, 1)
        count = 7 if group < 3 else 6
        for tap in range(count):
            grad_two[group * 7 + tap] = rows[tap * 16 : tap * 16 + 16, 0:32]
    for kd in range(3):
        for tap in range(9):
            at, lane0 = (tap, 0) if tap < 6 else (tap - 6, 48)
            piece = whole[112 + at * 4 : 116 + at * 4, :] * scale_one
            lane0 += 16 * kd
            if lane0:
                piece = pltpu.roll(piece, 128 - lane0, 1)
            grad_one[kd * 9 + tap] = piece[:, 0:16]
    row = whole[136:144, :]
    shift_two[...] = row[0:1, 0:32] * scale_two
    shift_one[...] = pltpu.roll(row, 96, 1)[0:1, 0:16] * scale_one


def in_vmem(count):
    return [pl.BlockSpec(memory_space=pltpu.VMEM)] * count


def run_layers(flags, *arrays):
    return pl.pallas_call(
        layers,
        out_shape=(
            jax.ShapeDtypeStruct((512, 128), BF16),
            jax.ShapeDtypeStruct((256, 128), BF16),
            jax.ShapeDtypeStruct((144, 128), F32),
        ),
        in_specs=[pl.BlockSpec(memory_space=pltpu.SMEM)] + in_vmem(len(arrays)),
        out_specs=(
            pl.BlockSpec(memory_space=pl.ANY),
            pl.BlockSpec(memory_space=pl.ANY),
            pl.BlockSpec(memory_space=pltpu.VMEM),
        ),
        scratch_shapes=[
            pltpu.VMEM((512, 128), BF16),
            pltpu.VMEM((256, 128), BF16),
            pltpu.SemaphoreType.DMA((2,)),
            pltpu.VMEM((4, 648, 128), F32),
            pltpu.VMEM((720, 2048), BF16),
            pltpu.VMEM((1152, 512), BF16),
            pltpu.VMEM((1728, 512), BF16),
            pltpu.VMEM((128, 2048), F32),
            pltpu.VMEM((128, 2048), BF16),
            pltpu.VMEM((528, 128), F32),
            pltpu.VMEM((528, 128), F32),
            pltpu.VMEM((272, 128), F32),
            pltpu.VMEM((448, 128), F32),
            pltpu.VMEM((48, 128), F32),
        ],
        compiler_params=pltpu.CompilerParams(vmem_limit_bytes=24 << 20),
        name="layers",
    )(flags, *arrays)


def run_edges(sample, target):
    return pl.pallas_call(
        edges,
        out_shape=(jax.ShapeDtypeStruct((28, 8, 256), BF16),) * 2,
        in_specs=[pl.BlockSpec(memory_space=pltpu.HBM)] * 2,
        out_specs=tuple(in_vmem(2)),
        scratch_shapes=[
            pltpu.VMEM((512, 128), BF16),
            pltpu.VMEM((528, 128), F32),
            pltpu.SemaphoreType.DMA((9,)),
        ],
        compiler_params=pltpu.CompilerParams(vmem_limit_bytes=4 << 20),
        name="edges",
    )(
        pltpu.with_memory_space_constraint(sample, pltpu.HBM),
        pltpu.with_memory_space_constraint(target, pltpu.HBM),
    )


def run_prepare(*filters):
    return pl.pallas_call(
        prepare,
        out_shape=(
            jax.ShapeDtypeStruct((256, 720), BF16),
            jax.ShapeDtypeStruct((64, 1), F32),
            jax.ShapeDtypeStruct((192, 1152), BF16),
            jax.ShapeDtypeStruct((32, 1), F32),
            jax.ShapeDtypeStruct((64, 1728), BF16),
        ),
        in_specs=in_vmem(4),
        out_specs=tuple(in_vmem(5)),
        scratch_shapes=[
            pltpu.VMEM((112, 128), F32),
            pltpu.VMEM((512, 128), F32),
            pltpu.VMEM((384, 128), F32),
        ],
        compiler_params=pltpu.CompilerParams(vmem_limit_bytes=4 << 20),
        name="prepare",
    )(*filters)


def run_unpack(scales, core_index, mine, other):
    return pl.pallas_call(
        functools.partial(unpack, *scales),
        out_shape=(
            jax.ShapeDtypeStruct((27, 4, 16), F32),
            jax.ShapeDtypeStruct((1, 16), F32),
            jax.ShapeDtypeStruct((27, 16, 32), F32),
            jax.ShapeDtypeStruct((1, 32), F32),
        ),
        in_specs=[pl.BlockSpec(memory_space=pltpu.SMEM)] + in_vmem(2),
        out_specs=tuple(in_vmem(4)),
        scratch_shapes=[pltpu.VMEM((144, 128), F32)],
        compiler_params=pltpu.CompilerParams(vmem_limit_bytes=4 << 20),
        name="unpack",
    )(core_index, mine, other)


def device_exchanges():
    def place(index):
        dp, space = divmod(index, 16)
        return [dp & 1, (dp >> 1) & 3, space & 3, (dp >> 3) * 4 + (space >> 2)]

    def index_of(core, x, y, z):
        return ((z >> 2) * 8 + x * 2 + core) * 16 + (z & 3) * 4 + y

    def pairing(*masks):
        pairs = []
        for index in range(256):
            spot = [at ^ mask for at, mask in zip(place(index), masks)]
            pairs.append((index, index_of(*spot)))
        return pairs

    fours = (
        (pairing(0, 0, 1, 0), pairing(0, 1, 0, 0), pairing(0, 1, 1, 0)),
        (pairing(0, 0, 3, 0), pairing(0, 3, 0, 0), pairing(0, 3, 3, 0)),
        (pairing(0, 0, 0, 1), pairing(0, 0, 0, 2), pairing(0, 0, 0, 3)),
    )
    return pairing(1, 0, 0, 0), fours, pairing(0, 0, 0, 7)


def add_up(grads, core_index):
    axes = ("dp", "space")
    core, fours, last = device_exchanges()
    low = core_index == 0
    top, bottom = grads[:72], grads[72:]
    mine = jnp.where(low, top, bottom) + lax.ppermute(jnp.where(low, bottom, top), axes, core)
    for first, second, third in fours:
        one, two, three = (lax.ppermute(mine, axes, pairs) for pairs in (first, second, third))
        mine = lax.optimization_barrier((mine + one) + (two + three))
    mine = mine + lax.ppermute(mine, axes, last)
    return mine, lax.ppermute(mine, axes, core)


def as_rows(first_filters, first_biases, second_filters, second_biases):
    return (
        first_filters.transpose(2, 3, 4, 1, 0).reshape(108, 16),
        first_biases[None],
        second_filters.transpose(2, 3, 4, 1, 0).reshape(432, 32),
        second_biases[None],
    )


def shards(volume, first_filters, first_biases, second_filters, second_biases, cotangent):
    sample, target = volume[0], cotangent[0]
    slabs = lax.axis_size("space")
    here = lax.axis_index("space")
    forward = [(i, i + 1) for i in range(slabs - 1)]
    backward = [(i + 1, i) for i in range(slabs - 1)]
    target = target.reshape(512, 128)
    upward, downward = run_edges(sample, target)
    below = lax.ppermute(upward, "space", forward)
    above = lax.ppermute(downward, "space", backward)
    matrices = run_prepare(*as_rows(first_filters, first_biases, second_filters, second_biases))
    flags = jnp.stack([here > 0, here < slabs - 1]).astype(F32)
    act, pooled_grad, grads = run_layers(flags, sample, below, above, target, *matrices)
    core_index = lax.axis_index("dp") % 2
    mine, other = add_up(grads, core_index)
    count_one = (
        lax.axis_size("dp") * slabs * PLANES * sample.shape[2] * sample.shape[3]
    )
    scales = (1.0 / math.sqrt(count_one), 1.0 / math.sqrt(count_one / 8))
    grad_one, shift_one, grad_two, shift_two = run_unpack(scales, core_index[None], mine, other)
    return (
        act.reshape(1, 32, 4, 4, 128),
        pooled_grad.reshape(1, 16, 4, 4, 128),
        grad_one.reshape(3, 3, 3, 4, 16).transpose(4, 3, 0, 1, 2),
        shift_one[0],
        grad_two.reshape(3, 3, 3, 16, 32).transpose(4, 3, 0, 1, 2),
        shift_two[0],
    )


def solution(mesh):
    slab = P("dp", None, "space", None, None)
    return jax.shard_map(
        shards,
        mesh=mesh,
        in_specs=(slab, P(), P(), P(), P(), slab),
        out_specs=(slab, slab, P(), P(), P(), P()),
        check_vma=False,
    )
```
